512 devices in a mesh: loc: 512 (over x, y, z, core).
Axes of the slice: x: 4, y: 4, z: 16, core: 2. Of those that a mesh axis runs over, the one named last changes fastest.
Arguments:
- points: float32 [3, 524288], P(None, 'loc'), may hold values from -1 to 1, as said below
- right_sides: float32 [16, 524288], P(None, 'loc')
- skeleton: int32 [8, 131072], P(None, 'loc'), may hold values from 0 to 1023, as said below
- lengthscale: float32 [1], replicated, may hold values from 0.026516505 to 0.06629126
- far_length: float32 [1], replicated, may hold values from 0.4 to 1
- signal: float32 [1], replicated, may hold values from 0.00024414062 to 0.0009765625
- noise_var: float32 [1], replicated, may hold values from 0.5 to 2
Outputs:
- solution: float32 [16, 524288], P(None, 'loc')
- residual: float32 [16, 524288], P(None, 'loc')
- slope_image: float32 [16, 524288], P(None, 'loc')
- trace_terms: float32 [16], replicated
The draws below stay inside these ranges and needn't reach their ends.
Inputs may be any that keep to these rules, and one draw needn't show every extreme that they name: `points`: unit vectors. `skeleton`: each leaf's 256 entries of a level rise, the j-th in the range j*1024/256 to (j+1)*1024/256 - 1.
All inputs are finite; a program needn't handle non-finite values.
Results may differ from the reference program's by a relative error of at most 0.002.
Values may be sent and summed in bfloat16 or wider, within the bound.
A program may use at most 64 MiB of HBM per device.

```python
import math
import jax
import jax.numpy as jnp
from jax import lax

ROWS = 1024
R = 256
PROBES = 16
ITERS = 2
NPTS = 524288
LEVELS = 8


def hilbert_cells(cell_ids, curve_order):
    column = jnp.zeros_like(cell_ids)
    row_pos = jnp.zeros_like(cell_ids)
    remain = cell_ids
    for level_id in range(curve_order):
        extent = 2 ** level_id
        flip_x = remain // 2 & 1
        flip_y = (remain ^ flip_x) & 1
        rotate = flip_y == 0
        mirror = rotate & (flip_x == 1)
        column_m = jnp.where(mirror, extent - 1 - column, column)
        row_m = jnp.where(mirror, extent - 1 - row_pos, row_pos)
        column = jnp.where(rotate, row_m, column_m) + extent * flip_x
        row_pos = jnp.where(rotate, column_m, row_m) + extent * flip_y
        remain = remain // 4
    return (column, row_pos)


def sphere_points(key):
    total_bits = NPTS.bit_length() - 1
    curve_order = (total_bits - 3) // 2
    side_cells = 2 ** curve_order
    point_ids = jnp.arange(NPTS, dtype=jnp.int32)
    cell_ids = point_ids // 2 ** (total_bits - 2 * curve_order)
    column, row_pos = hilbert_cells(cell_ids, curve_order)
    jitter = jax.random.uniform(key, (2, NPTS), jnp.float32)
    longitude = 2.0 * math.pi * (column.astype(jnp.float32) + jitter[0]) / side_cells - math.pi
    height = 2.0 * (row_pos.astype(jnp.float32) + jitter[1]) / side_cells - 1.0
    planar = jnp.sqrt(jnp.maximum(1.0 - height * height, 0.0))
    return jnp.stack([planar * jnp.cos(longitude), planar * jnp.sin(longitude), height])


def draw_points(key, part):
    return sphere_points(jax.random.fold_in(key, 11))


def draw_right_sides(key, part):
    locations = sphere_points(jax.random.fold_in(key, 11))
    keys_list = jax.random.split(jax.random.fold_in(key, 23), 4)
    rough = jnp.clip(jax.random.normal(keys_list[0], (PROBES, NPTS), jnp.float32), -4.0, 4.0)
    probe_scale = jnp.exp(jax.random.uniform(keys_list[1], (PROBES, 1), jnp.float32, 0.0, math.log(3.0)))
    smooth_weight = 2.0
    cell_scale = jnp.exp(jax.random.uniform(keys_list[2], (1, NPTS), jnp.float32, math.log(0.3), math.log(3.0)))
    tilts = jax.random.uniform(keys_list[3], (PROBES, 3), jnp.float32, -0.5, 0.5)
    smooth = 1.5 + tilts[:, 0:1] * locations[0][None, :] + tilts[:, 1:2] * locations[1][None, :] + tilts[:, 2:3] * locations[2][None, :]
    return probe_scale * (0.5 * cell_scale * rough + smooth_weight * smooth)


def draw_skeleton(key, part):
    stride = ROWS // R
    leaf_count = NPTS // ROWS
    offsets = jax.random.randint(key, (LEVELS, leaf_count, R), 0, stride, dtype=jnp.int32)
    starts = jnp.arange(R, dtype=jnp.int32) * stride
    return (starts[None, None, :] + offsets).reshape(LEVELS, leaf_count * R)


def setup_inputs(seed: int = 0) -> dict:
    streams_of = jax.random.split(jax.random.key(seed), 8)
    points = draw_points(jax.random.fold_in(streams_of[7], 71), 0)
    right_sides = draw_right_sides(jax.random.fold_in(streams_of[7], 71), 0)
    skeleton = draw_skeleton(jax.random.fold_in(streams_of[7], 71), 0)
    lengthscale = jnp.clip(jnp.exp(jax.random.uniform(streams_of[3], (1,), jnp.float32, math.log(0.026516505), math.log(0.06629126))), 0.026516505, 0.06629126)
    far_length = jnp.clip(jnp.exp(jax.random.uniform(streams_of[4], (1,), jnp.float32, math.log(0.4), math.log(1.0))), 0.4, 1.0)
    signal = jnp.clip(jnp.exp(jax.random.uniform(streams_of[5], (1,), jnp.float32, math.log(0.00024414062), math.log(0.0009765625))), 0.00024414062, 0.0009765625)
    noise_var = jnp.clip(jnp.exp(jax.random.uniform(streams_of[6], (1,), jnp.float32, math.log(0.5), math.log(2.0))), 0.5, 2.0)
    return {"points": points, "right_sides": right_sides, "skeleton": skeleton, "lengthscale": lengthscale, "far_length": far_length, "signal": signal, "noise_var": noise_var}


root_three = 1.7320508075688772

def kernel_pair(row_pts, col_pts, length):
    diff_a = row_pts[0][:, None] - col_pts[0][None, :]
    diff_b = row_pts[1][:, None] - col_pts[1][None, :]
    diff_c = row_pts[2][:, None] - col_pts[2][None, :]
    radius = jnp.sqrt(diff_a * diff_a + diff_b * diff_b + diff_c * diff_c)
    scaled = root_three * radius / length
    decay = jnp.exp(-scaled)
    return ((1.0 + scaled) * decay, scaled * scaled * decay)

def contract_rows(vectors, matrix):
    return lax.dot_general(vectors, matrix, (((1,), (1,)), ((), ())), preferred_element_type=jnp.float32)

def reference(points, right_sides, skeleton, lengthscale, far_length, signal, noise_var):
    length = lengthscale[0]
    far_len = far_length[0]
    signal_var = signal[0]
    nugget = noise_var[0]
    leaf_count = NPTS // ROWS
    leaf_pts = points.reshape(3, leaf_count, ROWS).transpose(1, 0, 2)
    blank_pts = jnp.zeros((1, 3, ROWS), jnp.float32)
    padded_pts = jnp.concatenate([blank_pts, leaf_pts, blank_pts], axis=0)
    skel_idx = skeleton.reshape(LEVELS, leaf_count, R)
    own_skel = []
    for level_id in range(LEVELS):
        picks = jnp.broadcast_to(skel_idx[level_id][:, None, :], (leaf_count, 3, R))
        own_skel.append(jnp.take_along_axis(leaf_pts, picks, axis=2))
    far_scale = 1.0 / (R * R * LEVELS)

    def apply_kernel(vectors, slope_rows):
        vec_count = vectors.shape[0]
        vec_half = vectors.astype(jnp.bfloat16)
        leaf_half = vec_half.reshape(vec_count, leaf_count, ROWS).transpose(1, 0, 2)
        blank_half = jnp.zeros((1, vec_count, ROWS), jnp.bfloat16)
        padded_half = jnp.concatenate([blank_half, leaf_half, blank_half], axis=0)

        def coef_leaf(leaf_id):
            coef_list = []
            for level_id in range(LEVELS):
                basis = kernel_pair(own_skel[level_id][leaf_id], leaf_pts[leaf_id], far_len)[0].astype(jnp.bfloat16)
                coef_list.append(contract_rows(leaf_half[leaf_id], basis))
            return jnp.stack(coef_list)
        coefs = lax.map(coef_leaf, jnp.arange(leaf_count, dtype=jnp.int32))

        def image_leaf(leaf_id):
            own_pts = leaf_pts[leaf_id]
            far_sum = jnp.zeros((vec_count, ROWS), jnp.float32)
            for level_id in range(LEVELS):
                partner_id = jnp.bitwise_xor(leaf_id, 1 << level_id + 1)
                basis = kernel_pair(own_skel[level_id][leaf_id], own_pts, far_len)[0].astype(jnp.bfloat16)
                coupling = kernel_pair(own_skel[level_id][partner_id], own_skel[level_id][leaf_id], far_len)[0]
                mixed_half = jnp.dot(coefs[partner_id, level_id], coupling, precision=lax.Precision.HIGHEST).astype(jnp.bfloat16)
                far_sum = far_sum + jnp.dot(mixed_half, basis, preferred_element_type=jnp.float32)
            near_sum = jnp.zeros((vec_count, ROWS), jnp.float32)
            slope_acc = jnp.zeros((max(slope_rows, 1), ROWS), jnp.float32)
            for offset in range(3):
                col_pts = padded_pts[leaf_id + offset]
                col_half = padded_half[leaf_id + offset]
                kernel_vals, slope_vals = kernel_pair(own_pts, col_pts, length)
                near_sum = near_sum + contract_rows(col_half, kernel_vals.astype(jnp.bfloat16))
                if slope_rows > 0:
                    slope_acc = slope_acc + contract_rows(col_half[:slope_rows], slope_vals.astype(jnp.bfloat16))
            return (near_sum + far_scale * far_sum, slope_acc)
        images, slopes = lax.map(image_leaf, jnp.arange(leaf_count, dtype=jnp.int32))
        images = images.transpose(1, 0, 2).reshape(vec_count, NPTS)
        slopes = slopes.transpose(1, 0, 2).reshape(slopes.shape[1], NPTS)
        return (images, slopes)
    ones_row = jnp.ones((1, NPTS), jnp.float32)
    first_out, slope_raw = apply_kernel(jnp.concatenate([right_sides, ones_row], axis=0), PROBES)
    row_sums = first_out[PROBES:]
    slope_image = signal_var * slope_raw

    def operate(vectors, kernel_part):
        return nugget * vectors + signal_var * (kernel_part + row_sums * vectors)
    image = operate(right_sides, first_out[:PROBES])
    solution = jnp.zeros_like(right_sides)
    residual = right_sides
    direction = right_sides
    norm_now = lax.optimization_barrier(jnp.sum(residual * residual, axis=1))
    for sweep in range(ITERS):
        if sweep > 0:
            image = operate(direction, apply_kernel(direction, 0)[0])
        alpha = norm_now / lax.optimization_barrier(jnp.sum(direction * image, axis=1))
        solution = solution + alpha[:, None] * direction
        residual = residual - alpha[:, None] * image
        norm_next = lax.optimization_barrier(jnp.sum(residual * residual, axis=1))
        direction = residual + (norm_next / norm_now)[:, None] * direction
        norm_now = norm_next
    trace_terms = lax.optimization_barrier(jnp.sum(solution * slope_image, axis=1)) / NPTS
    return (solution, residual, slope_image, trace_terms)
```

```python
import functools

import jax
import jax.numpy as jnp
from jax import lax
from jax.experimental import pallas as pl
from jax.experimental.pallas import tpu as pltpu
from jax.sharding import PartitionSpec as P

F32 = jnp.float32
BF = jnp.bfloat16
LOG2E = 1.4426950408889634
STRIDE = 4
LANES = 128
VROWS = 48
CROWS = 24
MESH = pl.DeviceIdType.MESH


def split2(x):
    hi = x.astype(BF)
    return hi, (x - hi.astype(F32)).astype(BF)


def split3(x):
    hi = x.astype(BF).astype(F32)
    rest = x - hi
    mid = rest.astype(BF).astype(F32)
    return hi, mid, rest - mid


def row_ids(shape):
    return lax.broadcasted_iota(jnp.int32, shape, 0)


def left_side(pts, scale, extra=None):
    rows = row_ids(pts.shape)
    square = scale * jnp.sum(pts * pts, axis=0, keepdims=True)
    full = jnp.where(rows < 3, -2.0 * scale * pts, jnp.where(rows == 3, square, jnp.where(rows == 4, scale, 0.0)))
    hi, mid, low = split3(full)
    parts = [hi, hi, hi, mid, mid, mid, low, low, low]
    if extra is not None:
        parts.append(extra)
    filler = jnp.zeros((LANES - 8 * len(parts), pts.shape[1]), F32)
    return jnp.concatenate(parts + [filler], axis=0)


def right_side(pts):
    rows = row_ids(pts.shape)
    square = jnp.sum(pts * pts, axis=0, keepdims=True)
    full = jnp.where(rows < 3, pts, jnp.where(rows == 3, 1.0, jnp.where(rows == 4, square, 0.0)))
    hi, mid, low = split3(full)
    filler = jnp.zeros((LANES - 72, pts.shape[1]), F32)
    return jnp.concatenate([hi, mid, low] * 3 + [filler], axis=0).astype(BF)


def matern(square, want_slope):
    square = jnp.maximum(square, 1e-30)
    scaled = square * lax.rsqrt(square)
    decay = jnp.exp2(scaled * (-LOG2E))
    first = scaled * decay
    if want_slope:
        return decay + first, scaled * first
    return decay + first


def dot(a, b):
    return jnp.dot(a, b, preferred_element_type=F32)


def dot_t(a, b):
    return lax.dot_general(a, b, (((1,), (1,)), ((), ())), preferred_element_type=F32)


def pack(columns):
    lanes = lax.broadcasted_iota(jnp.int32, (16, LANES), 1)
    rows = row_ids((16, LANES))
    total = jnp.zeros((16, LANES), F32)
    for k, column in enumerate(columns):
        total = jnp.where(lanes == rows + 16 * k, column, total)
    return jnp.sum(total, axis=0, keepdims=True)


def unpack(line, k):
    lanes = lax.broadcasted_iota(jnp.int32, (16, LANES), 1)
    rows = row_ids((16, LANES))
    return jnp.sum(jnp.where(lanes == rows + 16 * k, line, 0.0), axis=1, keepdims=True)


def row_dot(a, b):
    return jnp.sum(a * b, axis=1, keepdims=True)


def kernel(
    bits, groups, pts_ref, r0_ref, skel_ref, len_ref, far_ref, sig_ref, noise_ref,
    sol_ref, res_ref, slope_ref, trace_ref,
    p8, vec, qvec, nbp, nbr, at, a_near, a_far, b_own, kbuf, fbuf, psel, prec, chi, clo, grp,
    cs1, cr1, cs2, cr2, acc_k, acc_s, far_acc, q_buf, rs_buf, red_a, red_b,
    nb_send, nb_recv, q_send, q_recv, sk_send, sk_recv, c1_send, c1_recv, c2_send, c2_recv,
    ra_send, ra_recv, rb_send, rb_recv,
):
    n = 2**bits
    levels, rank = skel_ref.shape
    rows = pts_ref.shape[1]
    tile = rank
    tiles = rows // tile
    far_scale = 1.0 / (rank * rank * levels)
    me = lax.axis_index("loc")
    flip = [2**b * (1 - 2 * ((me // 2**b) % 2)) for b in range(bits)]
    right = (me + 1) % n
    left = (me + n - 1) % n
    group_a, group_b = groups

    def peers(group):
        found = []
        for d in range(1, 2 ** len(group)):
            found.append(me + sum(flip[b] for i, b in enumerate(group) if (d >> i) & 1))
        return found

    peers_a, peers_b = peers(group_a), peers(group_b)
    barrier = pltpu.get_barrier_semaphore()
    for peer in peers_a + peers_b + [left, right]:
        pl.semaphore_signal(barrier, inc=1, device_id=(peer,), device_id_type=MESH)

    def send(src, dst, ssem, rsem, peer):
        copy = pltpu.make_async_remote_copy(
            src_ref=src, dst_ref=dst, send_sem=ssem, recv_sem=rsem, device_id=(peer,), device_id_type=MESH
        )
        copy.start()
        return copy

    pending = []

    p8[...] = jnp.zeros_like(p8)
    p8[0:3, :] = pts_ref[...]
    raw = p8[...]
    centre = raw[:, 0:1]
    own = raw - centre
    near_scale = 3.0 / jnp.full((1, rows), len_ref[0] * len_ref[0], F32)
    far_scale2 = 3.0 / jnp.full((1, rows), far_ref[0] * far_ref[0], F32)
    b_own[...] = right_side(own)
    a_near[1] = left_side(own, near_scale).T.astype(BF)
    at[...] = left_side(own, far_scale2, raw).T
    picks = []
    for o in range(STRIDE):
        part = at[pl.ds(o, rank, stride=STRIDE), :]
        a_far[o] = part.astype(BF)
        picks.append(part.T[72:80, :])

    offs = skel_ref[...] - STRIDE * lax.broadcasted_iota(jnp.int32, skel_ref.shape, 1)

    def choose(level, values):
        off = offs[level : level + 1, :]
        result = values[0]
        for o in range(1, STRIDE):
            result = jnp.where(off == o, values[o], result)
        return result

    for level in range(levels):
        psel[level] = choose(level, picks)

    r0 = r0_ref[...]
    hi, low = split2(r0)
    vec[1, 0:16, :] = hi
    vec[1, 16:32, :] = low
    marks = jnp.where(row_ids((16, rows)) == 0, 1.0, 0.0)
    vec[1, 32:48, :] = marks.astype(BF)

    def far_chunk(o, carry):
        left_part = a_far[o]
        for j in range(tiles):
            cols = pl.ds(j * tile, tile)
            fbuf[o, :, cols] = matern(dot(left_part, b_own[:, cols]), False).astype(BF)
        grp[o] = dot_t(vec[1], fbuf[o])
        return carry

    lax.fori_loop(0, STRIDE, far_chunk, 0)

    parts = [grp[o] for o in range(STRIDE)]
    parts = [
        jnp.concatenate([g[0:16] + g[16:32], g[32:40]], axis=0)
        for g in parts
    ]
    for level in range(levels):
        cs1[level] = choose(level, parts)

    pl.semaphore_wait(barrier, len(peers_a) + len(peers_b) + 2)

    nb = [
        send(pts_ref, nbp.at[0], nb_send.at[0], nb_recv.at[0], right),
        send(pts_ref, nbp.at[1], nb_send.at[1], nb_recv.at[1], left),
        send(r0_ref, nbr.at[0], nb_send.at[2], nb_recv.at[2], right),
        send(r0_ref, nbr.at[1], nb_send.at[3], nb_recv.at[3], left),
    ]
    sk, c1 = [], []
    for level in range(levels):
        peer = me + flip[level + 1]
        sk.append(send(psel.at[level], prec.at[level], sk_send.at[level], sk_recv.at[level], peer))
        c1.append(send(cs1.at[level], cr1.at[level], c1_send.at[level], c1_recv.at[level], peer))
    pending += nb + sk + c1

    acc_k[...] = jnp.zeros_like(acc_k)
    acc_s[...] = jnp.zeros_like(acc_s)

    def near_block(slot):
        def chunk(i, carry):
            at_rows = pl.ds(pl.multiple_of(i * tile, tile), tile)
            left_part = a_near[slot, at_rows, :]
            head = vec[slot, :, at_rows]
            for j in range(tiles):
                cols = pl.ds(j * tile, tile)
                value, slope = matern(dot(left_part, b_own[:, cols]), True)
                value = value.astype(BF)
                kbuf[slot, at_rows, cols] = value
                acc_k[:, cols] += dot(head, value)
                acc_s[:, cols] += dot(head[0:16], slope.astype(BF))
            return carry

        lax.fori_loop(0, tiles, chunk, 0)

    near_block(1)
    valid = [jnp.where(me > 0, 1.0, 0.0), jnp.where(me < n - 1, 1.0, 0.0)]
    for side, slot in ((0, 0), (1, 2)):
        nb[side].wait_recv()
        nb[2 + side].wait_recv()
        p8[0:3, :] = nbp[side]
        a_near[slot] = left_side(p8[...] - centre, near_scale).T.astype(BF)
        hi, low = split2(nbr[side] * valid[side])
        vec[slot, 0:16, :] = hi
        vec[slot, 16:32, :] = low
        vec[slot, 32:48, :] = (marks * valid[side]).astype(BF)
        near_block(slot)

    side_scale = far_scale2[:, 0:rank]
    for level in range(levels):
        sk[level].wait_recv()
        a_side = left_side(prec[level] - centre, side_scale).T.astype(BF)
        b_side = right_side(psel[level] - centre)
        hi, low = split2(matern(dot(a_side, b_side), False))
        chi[level] = hi
        clo[level] = low

    def far_part(copies, received, rounded):
        count = received.shape[1]
        sums = [jnp.zeros((count, rank), F32) for _ in range(STRIDE)]
        for level in range(levels):
            copies[level].wait_recv()
            hi, low = split2(received[level])
            mixed = dot(hi, chi[level]) + dot(low, chi[level]) + dot(hi, clo[level])
            off = offs[level : level + 1, :]
            for o in range(STRIDE):
                sums[o] = sums[o] + jnp.where(off == o, mixed, 0.0)
        total = jnp.zeros((count, rows), F32)
        for o in range(STRIDE):
            hi, low = split2(sums[o])
            total = total + dot(hi, fbuf[o]) + dot(low, fbuf[o])
        return far_scale * total

    far_now = far_part(c1, cr1, True)
    near_now = acc_k[...]
    sig, noise = sig_ref[0], noise_ref[0]
    row_sums = near_now[32:33] + far_now[16:17]
    image = noise * r0 + sig * (near_now[0:16] + near_now[16:32] + far_now[0:16] + row_sums * r0)
    slope_image = sig * acc_s[...]
    slope_ref[...] = slope_image
    q_buf[...] = image
    rs_buf[...] = jnp.broadcast_to(row_sums, rs_buf.shape)
    hi, low = split2(image)
    qvec[1, 0:16, :] = hi
    qvec[1, 16:32, :] = low

    qs = [
        send(qvec.at[1], qvec.at[0], q_send.at[0], q_recv.at[0], right),
        send(qvec.at[1], qvec.at[2], q_send.at[1], q_recv.at[1], left),
    ]

    def start_reduce(step, line):
        red_a[step, 0] = line
        return [
            send(red_a.at[step, 0], red_a.at[step, d + 1], ra_send.at[step, d], ra_recv.at[step, d], peer)
            for d, peer in enumerate(peers_a)
        ]

    def halve(values):
        while values.shape[0] > 1:
            half = values.shape[0] // 2
            values = values[:half] + values[half:]
        return values[0]

    def middle_reduce(step, copies):
        for copy in copies:
            copy.wait_recv()
        red_b[step, 0] = halve(red_a[step])
        return [
            send(red_b.at[step, 0], red_b.at[step, d + 1], rb_send.at[step, d], rb_recv.at[step, d], peer)
            for d, peer in enumerate(peers_b)
        ]

    def end_reduce(step, copies):
        for copy in copies:
            copy.wait_recv()
        return halve(red_b[step])

    line = pack([row_dot(r0, r0), row_dot(r0, image), row_dot(r0, slope_image)])
    first_a = start_reduce(0, line)

    parts = []
    for o in range(STRIDE):
        g = dot_t(qvec[1], fbuf[o])
        parts.append(g[0:16] + g[16:32])
    for level in range(levels):
        cs2[level] = choose(level, parts)
    c2 = [
        send(cs2.at[level], cr2.at[level], c2_send.at[level], c2_recv.at[level], me + flip[level + 1])
        for level in range(levels)
    ]
    pending += qs + first_a + c2

    acc2 = dot(qvec[1], kbuf[1])
    first_b = middle_reduce(0, first_a)
    pending += first_b
    for side, slot in ((0, 0), (1, 2)):
        qs[side].wait_recv()
        acc2 = acc2 + valid[side] * dot(qvec[slot], kbuf[slot])
    far_now = far_part(c2, cr2, False)
    image = q_buf[...]
    second = noise * image + sig * (acc2[0:16] + acc2[16:32] + far_now + rs_buf[0:1, :] * image)

    line = end_reduce(0, first_b)
    norm0, inner0, start_slope = unpack(line, 0), unpack(line, 1), unpack(line, 2)
    alpha0 = norm0 / inner0
    slope_image = slope_ref[...]
    r0 = r0_ref[...]
    r1 = r0 - alpha0 * image
    r1_image = image - alpha0 * second
    line = pack(
        [
            row_dot(r1, r1),
            row_dot(r1, r1_image),
            row_dot(r1, image) + row_dot(r0, r1_image),
            row_dot(r1, slope_image),
        ]
    )
    second_a = start_reduce(1, line)
    second_b = middle_reduce(1, second_a)
    line = end_reduce(1, second_b)
    pending += second_a + second_b
    norm1, inner1, cross1, slope1 = [unpack(line, k) for k in range(4)]
    beta = norm1 / norm0
    inner1 = inner1 + beta * (cross1 + beta * inner0)
    alpha1 = norm1 / inner1
    direction = r1 + beta * r0
    sol_ref[...] = alpha0 * r0 + alpha1 * direction
    res_ref[...] = r1 - alpha1 * (r1_image + beta * image)
    trace = (alpha0 * start_slope + alpha1 * (slope1 + beta * start_slope)) * (1.0 / (n * rows))
    trace_ref[...] = pack([trace])
    for copy in pending:
        copy.wait_send()


def shards(points, right_sides, skeleton, lengthscale, far_length, signal, noise_var):
    n = lax.axis_size("loc")
    bits = n.bit_length() - 1
    rows = points.shape[1]
    levels, rank = skeleton.shape
    split = min(5, bits // 2 + 1)
    groups = (tuple(range(split)), tuple(range(split, bits)))
    size_a, size_b = 2 ** len(groups[0]), 2 ** len(groups[1])
    vmem = pl.BlockSpec(memory_space=pltpu.VMEM)
    smem = pl.BlockSpec(memory_space=pltpu.SMEM)
    dma = pltpu.SemaphoreType.DMA
    scratch = [
        pltpu.VMEM((8, rows), F32),
        pltpu.VMEM((3, VROWS, rows), BF),
        pltpu.VMEM((3, 32, rows), BF),
        pltpu.VMEM((2, 3, rows), F32),
        pltpu.VMEM((2, 16, rows), F32),
        pltpu.VMEM((rows, LANES), F32),
        pltpu.VMEM((3, rows, LANES), BF),
        pltpu.VMEM((STRIDE, rank, LANES), BF),
        pltpu.VMEM((LANES, rows), BF),
        pltpu.VMEM((3, rows, rows), BF),
        pltpu.VMEM((STRIDE, rank, rows), BF),
        pltpu.VMEM((levels, 8, rank), F32),
        pltpu.VMEM((levels, 8, rank), F32),
        pltpu.VMEM((levels, rank, rank), BF),
        pltpu.VMEM((levels, rank, rank), BF),
        pltpu.VMEM((STRIDE, VROWS, rank), F32),
        pltpu.VMEM((levels, CROWS, rank), F32),
        pltpu.VMEM((levels, CROWS, rank), F32),
        pltpu.VMEM((levels, 16, rank), F32),
        pltpu.VMEM((levels, 16, rank), F32),
        pltpu.VMEM((VROWS, rows), F32),
        pltpu.VMEM((16, rows), F32),
        pltpu.VMEM((16, rows), F32),
        pltpu.VMEM((16, rows), F32),
        pltpu.VMEM((8, rows), F32),
        pltpu.VMEM((2, size_a, 1, LANES), F32),
        pltpu.VMEM((2, size_b, 1, LANES), F32),
        dma((4,)), dma((4,)), dma((2,)), dma((2,)),
        dma((levels,)), dma((levels,)), dma((levels,)), dma((levels,)), dma((levels,)), dma((levels,)),
        dma((2, size_a - 1)), dma((2, size_a - 1)), dma((2, size_b - 1)), dma((2, size_b - 1)),
    ]
    block = jax.ShapeDtypeStruct(right_sides.shape, F32)
    outs = pl.pallas_call(
        functools.partial(kernel, bits, groups),
        out_shape=(block, block, block, jax.ShapeDtypeStruct((1, LANES), F32)),
        in_specs=[vmem] * 3 + [smem] * 4,
        out_specs=(vmem,) * 4,
        scratch_shapes=scratch,
        compiler_params=pltpu.CompilerParams(collective_id=0, has_side_effects=True, vmem_limit_bytes=48 * 2**20),
        name="cg",
    )(points, right_sides, skeleton, lengthscale, far_length, signal, noise_var)
    return outs[0], outs[1], outs[2], outs[3][0, : right_sides.shape[0]]


def solution(mesh):
    placed = (P(None, "loc"), P(None, "loc"), P(None, "loc"), P(), P(), P(), P())
    return jax.shard_map(
        shards,
        mesh=mesh,
        in_specs=placed,
        out_specs=(P(None, "loc"), P(None, "loc"), P(None, "loc"), P()),
        check_vma=False,
    )
```

```python
import functools

import jax
import jax.numpy as jnp
from jax import lax
from jax.experimental import pallas as pl
from jax.experimental.pallas import tpu as pltpu
from jax.sharding import PartitionSpec as P

F32 = jnp.float32
BF = jnp.bfloat16
LOG2E = 1.4426950408889634
STRIDE = 4
LANES = 128
VROWS = 48
MESH = pl.DeviceIdType.MESH


def split2(x):
    hi = x.astype(BF)
    return hi, (x - hi.astype(F32)).astype(BF)


def split3(x):
    hi = x.astype(BF).astype(F32)
    rest = x - hi
    mid = rest.astype(BF).astype(F32)
    return hi, mid, rest - mid


def row_ids(shape):
    return lax.broadcasted_iota(jnp.int32, shape, 0)


def left_side(pts, scale, extra=None):
    rows = row_ids(pts.shape)
    square = scale * jnp.sum(pts * pts, axis=0, keepdims=True)
    full = jnp.where(rows < 3, -2.0 * scale * pts, jnp.where(rows == 3, square, jnp.where(rows == 4, scale, 0.0)))
    hi, mid, low = split3(full)
    parts = [hi, hi, hi, mid, mid, mid, low, low, low]
    if extra is not None:
        parts.append(extra)
    filler = jnp.zeros((LANES - 8 * len(parts), pts.shape[1]), F32)
    return jnp.concatenate(parts + [filler], axis=0)


def right_side(pts):
    rows = row_ids(pts.shape)
    square = jnp.sum(pts * pts, axis=0, keepdims=True)
    full = jnp.where(rows < 3, pts, jnp.where(rows == 3, 1.0, jnp.where(rows == 4, square, 0.0)))
    hi, mid, low = split3(full)
    filler = jnp.zeros((LANES - 72, pts.shape[1]), F32)
    return jnp.concatenate([hi, mid, low] * 3 + [filler], axis=0).astype(BF)


def matern(square, want_slope):
    square = jnp.maximum(square, 1e-30)
    scaled = square * lax.rsqrt(square)
    decay = jnp.exp2(scaled * (-LOG2E))
    first = scaled * decay
    if want_slope:
        return decay + first, scaled * first
    return decay + first


def dot(a, b):
    return jnp.dot(a, b, preferred_element_type=F32)


def dot_t(a, b):
    return lax.dot_general(a, b, (((1,), (1,)), ((), ())), preferred_element_type=F32)


def pack(columns):
    lanes = lax.broadcasted_iota(jnp.int32, (16, LANES), 1)
    rows = row_ids((16, LANES))
    total = jnp.zeros((16, LANES), F32)
    for k, column in enumerate(columns):
        total = jnp.where(lanes == rows + 16 * k, column, total)
    return jnp.sum(total, axis=0, keepdims=True)


def unpack(line, k):
    lanes = lax.broadcasted_iota(jnp.int32, (16, LANES), 1)
    rows = row_ids((16, LANES))
    return jnp.sum(jnp.where(lanes == rows + 16 * k, line, 0.0), axis=1, keepdims=True)


def row_dot(a, b):
    return jnp.sum(a * b, axis=1, keepdims=True)


def kernel(
    bits, groups, pts_hbm, r0_hbm, skel_hbm, len_ref, far_ref, sig_ref, noise_ref,
    r1_ref, r1_image_ref, q_buf, slope_ref, first_ref, last_ref,
    pts_ref, r0_ref, skel_ref, in_sem, p8, vec, qvec, nbp, nbr, at, a_near, a_far, b_own, kbuf, fbuf, psel, prec, chi, clo, grp,
    cs1, cr1, cs2, cr2, acc_k, rs_buf, red_a, red_b,
    nb_send, nb_recv, q_send, q_recv, sk_send, sk_recv, c1_send, c1_recv, c2_send, c2_recv,
    ra_send, ra_recv, rb_send, rb_recv,
):
    n = 2**bits
    levels, rank = skel_ref.shape
    rows = pts_ref.shape[1]
    tile = rank
    tiles = rows // tile
    far_scale = 1.0 / (rank * rank * levels)
    loads = [
        pltpu.make_async_copy(src, dst, in_sem.at[i])
        for i, (src, dst) in enumerate(((pts_hbm, pts_ref), (skel_hbm, skel_ref), (r0_hbm, r0_ref)))
    ]
    for load in loads:
        load.start()
    me = lax.axis_index("loc")
    flip = [2**b * (1 - 2 * ((me // 2**b) % 2)) for b in range(bits)]
    right = (me + 1) % n
    left = (me + n - 1) % n
    group_a, group_b = groups

    def peers(group):
        found = []
        for d in range(1, 2 ** len(group)):
            found.append(me + sum(flip[b] for i, b in enumerate(group) if (d >> i) & 1))
        return found

    peers_a, peers_b = peers(group_a), peers(group_b)
    barrier = pltpu.get_barrier_semaphore()
    for peer in peers_a + peers_b + [left, right]:
        pl.semaphore_signal(barrier, inc=1, device_id=(peer,), device_id_type=MESH)

    def send(src, dst, ssem, rsem, peer):
        copy = pltpu.make_async_remote_copy(
            src_ref=src, dst_ref=dst, send_sem=ssem, recv_sem=rsem, device_id=(peer,), device_id_type=MESH
        )
        copy.start()
        return copy

    order = sorted(range(levels), key=lambda level: -(2**level if level < 4 else 2 ** (level % 2)))

    p8[...] = jnp.zeros_like(p8)
    loads[0].wait()
    p8[0:3, :] = pts_ref[...]
    raw = p8[...]
    centre = raw[:, 0:1]
    own = raw - centre
    near_scale = 3.0 / jnp.full((1, rows), len_ref[0] * len_ref[0], F32)
    far_scale2 = 3.0 / jnp.full((1, rows), far_ref[0] * far_ref[0], F32)
    b_own[...] = right_side(own)
    a_near[1] = left_side(own, near_scale).T.astype(BF)
    at[...] = left_side(own, far_scale2, raw).T
    picks = []
    for o in range(STRIDE):
        part = at[pl.ds(o, rank, stride=STRIDE), :]
        a_far[o] = part.astype(BF)
        picks.append(part.T[72:80, :])

    loads[1].wait()
    offs = skel_ref[...] - STRIDE * lax.broadcasted_iota(jnp.int32, skel_ref.shape, 1)

    def choose(level, values):
        off = offs[level : level + 1, :]
        result = values[0]
        for o in range(1, STRIDE):
            result = jnp.where(off == o, values[o], result)
        return result

    for level in range(levels):
        psel[level, 0:3, :] = choose(level, picks)[0:3]

    loads[2].wait()
    r0 = r0_ref[...]
    hi, low = split2(r0)
    vec[1, 0:16, :] = hi
    vec[1, 16:32, :] = low
    marks = jnp.where(row_ids((16, rows)) == 0, 1.0, 0.0)
    vec[1, 32:48, :] = marks.astype(BF)

    def far_chunk(o, carry):
        left_part = a_far[o]
        for j in range(tiles):
            cols = pl.ds(j * tile, tile)
            fbuf[o, :, cols] = matern(dot(left_part, b_own[:, cols]), False).astype(BF)
        grp[o] = dot_t(vec[1], fbuf[o])
        return carry

    lax.fori_loop(0, STRIDE, far_chunk, 0)

    parts = [grp[o] for o in range(STRIDE)]
    sums = [g[0:16] + g[16:32] for g in parts]
    ones = [g[32:33] for g in parts]
    for level in order:
        cs1[level] = choose(level, sums)
        psel[level, 3:4, :] = choose(level, ones)

    pl.semaphore_wait(barrier, len(peers_a) + len(peers_b) + 2)

    sk, c1 = {}, {}
    for i, level in enumerate(order):
        peer = me + flip[level + 1]
        sk[level] = send(psel.at[level], prec.at[level], sk_send.at[level], sk_recv.at[level], peer)
        c1[level] = send(cs1.at[level], cr1.at[level], c1_send.at[level], c1_recv.at[level], peer)
        if i == min(1, levels - 1):
            nb = [
                send(pts_ref, nbp.at[0], nb_send.at[0], nb_recv.at[0], right),
                send(pts_ref, nbp.at[1], nb_send.at[1], nb_recv.at[1], left),
                send(r0_ref, nbr.at[0], nb_send.at[2], nb_recv.at[2], right),
                send(r0_ref, nbr.at[1], nb_send.at[3], nb_recv.at[3], left),
            ]

    acc_k[...] = jnp.zeros_like(acc_k)
    slope_ref[...] = jnp.zeros_like(slope_ref)

    def near_block(slot):
        def chunk(i, carry):
            at_rows = pl.ds(pl.multiple_of(i * tile, tile), tile)
            left_part = a_near[slot, at_rows, :]
            head = vec[slot, :, at_rows]
            for j in range(tiles):
                cols = pl.ds(j * tile, tile)
                value, slope = matern(dot(left_part, b_own[:, cols]), True)
                value = value.astype(BF)
                kbuf[slot, at_rows, cols] = value
                acc_k[:, cols] += dot(head, value)
                slope_ref[:, cols] += dot(head[0:16], slope.astype(BF))
            return carry

        lax.fori_loop(0, tiles, chunk, 0)

    near_block(1)
    valid = [jnp.where(me > 0, 1.0, 0.0), jnp.where(me < n - 1, 1.0, 0.0)]
    for side, slot in ((0, 0), (1, 2)):
        nb[side].wait_recv()
        nb[2 + side].wait_recv()
        p8[0:3, :] = nbp[side]
        a_near[slot] = left_side(p8[...] - centre, near_scale).T.astype(BF)
        hi, low = split2(nbr[side] * valid[side])
        vec[slot, 0:16, :] = hi
        vec[slot, 16:32, :] = low
        vec[slot, 32:48, :] = (marks * valid[side]).astype(BF)
        near_block(slot)

    side_scale = far_scale2[:, 0:rank]

    def centred(four):
        full = jnp.concatenate([four, jnp.zeros_like(four)], axis=0)
        return jnp.where(row_ids(full.shape) < 3, full - centre, 0.0)

    for level in reversed(order):
        sk[level].wait_recv()
        a_side = left_side(centred(prec[level]), side_scale).T.astype(BF)
        b_side = right_side(centred(psel[level]))
        hi, low = split2(matern(dot(a_side, b_side), False))
        chi[level] = hi
        clo[level] = low

    def far_part(copies, received, with_ones):
        count = 24 if with_ones else 16
        sums = [jnp.zeros((count, rank), F32) for _ in range(STRIDE)]
        for level in reversed(order):
            copies[level].wait_recv()
            coef = received[level]
            if with_ones:
                tail = jnp.where(row_ids((8, rank)) == 0, prec[level, 3:4, :], 0.0)
                coef = jnp.concatenate([coef, tail], axis=0)
            hi, low = split2(coef)
            both = dot(jnp.concatenate([hi, low], axis=0), chi[level])
            mixed = both[:count] + both[count:] + dot(hi, clo[level])
            off = offs[level : level + 1, :]
            for o in range(STRIDE):
                sums[o] = sums[o] + jnp.where(off == o, mixed, 0.0)
        total = jnp.zeros((2 * count, rows), F32)
        for o in range(STRIDE):
            total = total + dot(jnp.concatenate(split2(sums[o]), axis=0), fbuf[o])
        return far_scale * (total[:count] + total[count:])

    far_now = far_part(c1, cr1, True)
    near_now = acc_k[...]
    sig, noise = sig_ref[0], noise_ref[0]
    row_sums = near_now[32:33] + far_now[16:17]
    image = noise * r0 + sig * (near_now[0:16] + near_now[16:32] + far_now[0:16] + row_sums * r0)
    slope_image = sig * slope_ref[...]
    slope_ref[...] = slope_image
    q_buf[...] = image
    rs_buf[...] = jnp.broadcast_to(row_sums, rs_buf.shape)
    hi, low = split2(image)
    qvec[1, 0:16, :] = hi
    qvec[1, 16:32, :] = low

    qs = [
        send(qvec.at[1], qvec.at[0], q_send.at[0], q_recv.at[0], right),
        send(qvec.at[1], qvec.at[2], q_send.at[1], q_recv.at[1], left),
    ]

    def start_reduce(step, line):
        red_a[step, 0] = line
        return [
            send(red_a.at[step, 0], red_a.at[step, d + 1], ra_send.at[step, d], ra_recv.at[step, d], peer)
            for d, peer in enumerate(peers_a)
        ]

    def halve(values):
        while values.shape[0] > 1:
            half = values.shape[0] // 2
            values = values[:half] + values[half:]
        return values[0]

    def middle_reduce(step, copies):
        for copy in copies:
            copy.wait_recv()
        red_b[step, 0] = halve(red_a[step])
        return [
            send(red_b.at[step, 0], red_b.at[step, d + 1], rb_send.at[step, d], rb_recv.at[step, d], peer)
            for d, peer in enumerate(peers_b)
        ]

    def end_reduce(step, copies):
        for copy in copies:
            copy.wait_recv()
        return halve(red_b[step])

    line = pack([row_dot(r0, r0), row_dot(r0, image), row_dot(r0, slope_image)])
    first_a = start_reduce(0, line)

    parts = []
    for o in range(STRIDE):
        g = dot_t(qvec[1], fbuf[o])
        parts.append(g[0:16] + g[16:32])
    c2 = {}
    for level in order:
        cs2[level] = choose(level, parts)
        peer = me + flip[level + 1]
        c2[level] = send(cs2.at[level], cr2.at[level], c2_send.at[level], c2_recv.at[level], peer)

    acc2 = dot(qvec[1], kbuf[1])
    first_b = middle_reduce(0, first_a)
    for copy in nb + list(sk.values()) + list(c1.values()):
        copy.wait_send()
    for side, slot in ((0, 0), (1, 2)):
        qs[side].wait_recv()
        acc2 = acc2 + valid[side] * dot(qvec[slot], kbuf[slot])
    far_now = far_part(c2, cr2, False)
    image = q_buf[...]
    second = noise * image + sig * (acc2[0:16] + acc2[16:32] + far_now + rs_buf[0:1, :] * image)

    line = end_reduce(0, first_b)
    first_ref[...] = line
    alpha0 = unpack(line, 0) / unpack(line, 1)
    slope_image = slope_ref[...]
    r0 = r0_ref[...]
    r1 = r0 - alpha0 * image
    r1_image = image - alpha0 * second
    line = pack(
        [
            row_dot(r1, r1),
            row_dot(r1, r1_image),
            row_dot(r1, image) + row_dot(r0, r1_image),
            row_dot(r1, slope_image),
        ]
    )
    second_a = start_reduce(1, line)
    r1_ref[...] = r1
    r1_image_ref[...] = r1_image
    for copy in qs + first_a + list(c2.values()) + first_b:
        copy.wait_send()
    second_b = middle_reduce(1, second_a)
    for copy in second_a:
        copy.wait_send()
    last_ref[...] = end_reduce(1, second_b)
    for copy in second_b:
        copy.wait_send()


def finish(scale, r1_ref, r1_image_ref, q_ref, slope_ref, first_ref, last_ref,
           sol_hbm, res_hbm, slope_hbm, trace_hbm, sol, res, trace_buf, sem):
    outs = [
        pltpu.make_async_copy(src, dst, sem.at[i])
        for i, (src, dst) in enumerate(
            ((slope_ref, slope_hbm), (sol, sol_hbm), (res, res_hbm), (trace_buf, trace_hbm))
        )
    ]
    outs[0].start()
    first, last = first_ref[...], last_ref[...]
    norm0, inner0, start_slope = unpack(first, 0), unpack(first, 1), unpack(first, 2)
    norm1, inner1, cross1, slope1 = [unpack(last, k) for k in range(4)]
    alpha0 = norm0 / inner0
    beta = norm1 / norm0
    alpha1 = norm1 / (inner1 + beta * (cross1 + beta * inner0))
    r1, q = r1_ref[...], q_ref[...]
    sol[...] = (alpha0 + alpha1 * beta) * (r1 + alpha0 * q) + alpha1 * r1
    outs[1].start()
    res[...] = r1 - alpha1 * (r1_image_ref[...] + beta * q)
    outs[2].start()
    trace = (alpha0 * start_slope + alpha1 * (slope1 + beta * start_slope)) * scale
    trace_buf[...] = pack([trace])[:, 0:16]
    outs[3].start()
    for out in outs:
        out.wait()


def shards(points, right_sides, skeleton, lengthscale, far_length, signal, noise_var):
    n = lax.axis_size("loc")
    bits = n.bit_length() - 1
    rows = points.shape[1]
    levels, rank = skeleton.shape
    split = min(5, bits // 2 + 1)
    groups = (tuple(range(split)), tuple(range(split, bits)))
    size_a, size_b = 2 ** len(groups[0]), 2 ** len(groups[1])
    vmem = pl.BlockSpec(memory_space=pltpu.VMEM)
    smem = pl.BlockSpec(memory_space=pltpu.SMEM)
    dma = pltpu.SemaphoreType.DMA
    hbm = pl.BlockSpec(memory_space=pltpu.HBM)
    scratch = [
        pltpu.VMEM((3, rows), F32),
        pltpu.VMEM((16, rows), F32),
        pltpu.VMEM((levels, rank), jnp.int32),
        dma((3,)),
        pltpu.VMEM((8, rows), F32),
        pltpu.VMEM((3, VROWS, rows), BF),
        pltpu.VMEM((3, 32, rows), BF),
        pltpu.VMEM((2, 3, rows), F32),
        pltpu.VMEM((2, 16, rows), F32),
        pltpu.VMEM((rows, LANES), F32),
        pltpu.VMEM((3, rows, LANES), BF),
        pltpu.VMEM((STRIDE, rank, LANES), BF),
        pltpu.VMEM((LANES, rows), BF),
        pltpu.VMEM((3, rows, rows), BF),
        pltpu.VMEM((STRIDE, rank, rows), BF),
        pltpu.VMEM((levels, 4, rank), F32),
        pltpu.VMEM((levels, 4, rank), F32),
        pltpu.VMEM((levels, rank, rank), BF),
        pltpu.VMEM((levels, rank, rank), BF),
        pltpu.VMEM((STRIDE, VROWS, rank), F32),
        pltpu.VMEM((levels, 16, rank), F32),
        pltpu.VMEM((levels, 16, rank), F32),
        pltpu.VMEM((levels, 16, rank), F32),
        pltpu.VMEM((levels, 16, rank), F32),
        pltpu.VMEM((VROWS, rows), F32),
        pltpu.VMEM((8, rows), F32),
        pltpu.VMEM((2, size_a, 1, LANES), F32),
        pltpu.VMEM((2, size_b, 1, LANES), F32),
        dma((4,)), dma((4,)), dma((2,)), dma((2,)),
        dma((levels,)), dma((levels,)), dma((levels,)), dma((levels,)), dma((levels,)), dma((levels,)),
        dma((2, size_a - 1)), dma((2, size_a - 1)), dma((2, size_b - 1)), dma((2, size_b - 1)),
    ]
    block = jax.ShapeDtypeStruct(right_sides.shape, F32)
    row = jax.ShapeDtypeStruct((1, LANES), F32)
    parts = pl.pallas_call(
        functools.partial(kernel, bits, groups),
        out_shape=(block,) * 4 + (row,) * 2,
        in_specs=[hbm] * 3 + [smem] * 4,
        out_specs=(vmem,) * 6,
        scratch_shapes=scratch,
        compiler_params=pltpu.CompilerParams(collective_id=0, has_side_effects=True, vmem_limit_bytes=56_200_000),
        name="cg",
    )(points, right_sides, skeleton, lengthscale, far_length, signal, noise_var)
    probes = right_sides.shape[0]
    outs = pl.pallas_call(
        functools.partial(finish, 1.0 / (n * rows)),
        out_shape=(block, block, block, jax.ShapeDtypeStruct((1, probes), F32)),
        in_specs=[vmem] * 6,
        out_specs=(hbm,) * 4,
        scratch_shapes=[
            pltpu.VMEM(right_sides.shape, F32), pltpu.VMEM(right_sides.shape, F32), pltpu.VMEM((1, probes), F32), dma((4,)),
        ],
        compiler_params=pltpu.CompilerParams(vmem_limit_bytes=2 * 2**20),
        name="finish",
    )(*parts)
    return outs[0], outs[1], outs[2], outs[3].reshape(probes)


def solution(mesh):
    placed = (P(None, "loc"), P(None, "loc"), P(None, "loc"), P(), P(), P(), P())
    return jax.shard_map(
        shards,
        mesh=mesh,
        in_specs=placed,
        out_specs=(P(None, "loc"), P(None, "loc"), P(None, "loc"), P()),
        check_vma=False,
    )
```

```python
import functools

import jax
import jax.numpy as jnp
from jax import lax
from jax.experimental import pallas as pl
from jax.experimental.pallas import tpu as pltpu
from jax.sharding import PartitionSpec as P

F32 = jnp.float32
BF = jnp.bfloat16
LOG2E = 1.4426950408889634
STRIDE = 4
LANES = 128
VROWS = 48
MESH = pl.DeviceIdType.MESH


def split2(x):
    hi = x.astype(BF)
    return hi, (x - hi.astype(F32)).astype(BF)


def split3(x):
    hi = x.astype(BF).astype(F32)
    rest = x - hi
    mid = rest.astype(BF).astype(F32)
    return hi, mid, rest - mid


def row_ids(shape):
    return lax.broadcasted_iota(jnp.int32, shape, 0)


def left_side(pts, scale, extra=None):
    rows = row_ids(pts.shape)
    square = scale * jnp.sum(pts * pts, axis=0, keepdims=True)
    full = jnp.where(rows < 3, -2.0 * scale * pts, jnp.where(rows == 3, square, jnp.where(rows == 4, scale, 0.0)))
    hi, mid, low = split3(full)
    parts = [hi, hi, hi, mid, mid, mid, low, low, low]
    if extra is not None:
        parts.append(extra)
    filler = jnp.zeros((LANES - 8 * len(parts), pts.shape[1]), F32)
    return jnp.concatenate(parts + [filler], axis=0)


def right_side(pts):
    rows = row_ids(pts.shape)
    square = jnp.sum(pts * pts, axis=0, keepdims=True)
    full = jnp.where(rows < 3, pts, jnp.where(rows == 3, 1.0, jnp.where(rows == 4, square, 0.0)))
    hi, mid, low = split3(full)
    filler = jnp.zeros((LANES - 72, pts.shape[1]), F32)
    return jnp.concatenate([hi, mid, low] * 3 + [filler], axis=0).astype(BF)


def matern(square, want_slope):
    square = jnp.maximum(square, 1e-30)
    scaled = square * lax.rsqrt(square)
    decay = jnp.exp2(scaled * (-LOG2E))
    first = scaled * decay
    if want_slope:
        return decay + first, scaled * first
    return decay + first


def dot(a, b):
    return jnp.dot(a, b, preferred_element_type=F32)


def dot_t(a, b):
    return lax.dot_general(a, b, (((1,), (1,)), ((), ())), preferred_element_type=F32)


def pack(columns):
    lanes = lax.broadcasted_iota(jnp.int32, (16, LANES), 1)
    rows = row_ids((16, LANES))
    total = jnp.zeros((16, LANES), F32)
    for k, column in enumerate(columns):
        total = jnp.where(lanes == rows + 16 * k, column, total)
    return jnp.sum(total, axis=0, keepdims=True)


def unpack(line, k):
    lanes = lax.broadcasted_iota(jnp.int32, (16, LANES), 1)
    rows = row_ids((16, LANES))
    return jnp.sum(jnp.where(lanes == rows + 16 * k, line, 0.0), axis=1, keepdims=True)


def row_dot(a, b):
    return jnp.sum(a * b, axis=1, keepdims=True)


def kernel(
    bits, groups, pts_hbm, r0_hbm, skel_hbm, len_ref, far_ref, sig_ref, noise_ref,
    r1_ref, r1_image_ref, q_buf, slope_ref, first_ref, last_ref,
    pts_ref, r0_ref, skel_ref, in_sem, p8, vec, qvec, nbp, nbr, at, a_near, a_far, b_own, kbuf, fbuf, psel, prec, chi, clo, grp,
    cs1, cr1, cs2, cr2, acc_k, rs_buf, red_a, red_b,
    nb_send, nb_recv, q_send, q_recv, sk_send, sk_recv, c1_send, c1_recv, c2_send, c2_recv,
    ra_send, ra_recv, rb_send, rb_recv,
):
    n = 2**bits
    levels, rank = skel_ref.shape
    rows = pts_ref.shape[1]
    tile = rank
    tiles = rows // tile
    far_scale = 1.0 / (rank * rank * levels)
    loads = [
        pltpu.make_async_copy(src, dst, in_sem.at[i])
        for i, (src, dst) in enumerate(((pts_hbm, pts_ref), (skel_hbm, skel_ref), (r0_hbm, r0_ref)))
    ]
    for load in loads:
        load.start()
    me = lax.axis_index("loc")
    flip = [2**b * (1 - 2 * ((me // 2**b) % 2)) for b in range(bits)]
    right = (me + 1) % n
    left = (me + n - 1) % n
    group_a, group_b = groups

    def peers(group):
        found = []
        for d in range(1, 2 ** len(group)):
            found.append(me + sum(flip[b] for i, b in enumerate(group) if (d >> i) & 1))
        return found

    peers_a, peers_b = peers(group_a), peers(group_b)
    barrier = pltpu.get_barrier_semaphore()
    for peer in peers_a + peers_b + [left, right]:
        pl.semaphore_signal(barrier, inc=1, device_id=(peer,), device_id_type=MESH)

    def send(src, dst, ssem, rsem, peer):
        copy = pltpu.make_async_remote_copy(
            src_ref=src, dst_ref=dst, send_sem=ssem, recv_sem=rsem, device_id=(peer,), device_id_type=MESH
        )
        copy.start()
        return copy

    def start_reduce(step, line):
        red_a[step, 0] = line
        return [
            send(red_a.at[step, 0], red_a.at[step, d + 1], ra_send.at[step, d], ra_recv.at[step, d], peer)
            for d, peer in enumerate(peers_a)
        ]

    def halve(values):
        while values.shape[0] > 1:
            half = values.shape[0] // 2
            values = values[:half] + values[half:]
        return values[0]

    def middle_reduce(step, copies):
        for copy in copies:
            copy.wait_recv()
        red_b[step, 0] = halve(red_a[step])
        return [
            send(red_b.at[step, 0], red_b.at[step, d + 1], rb_send.at[step, d], rb_recv.at[step, d], peer)
            for d, peer in enumerate(peers_b)
        ]

    def end_reduce(step, copies):
        for copy in copies:
            copy.wait_recv()
        return halve(red_b[step])

    order = sorted(range(levels), key=lambda level: -(2**level if level < 4 else 2 ** (level % 2)))

    p8[...] = jnp.zeros_like(p8)
    loads[0].wait()
    p8[0:3, :] = pts_ref[...]
    raw = p8[...]
    centre = raw[:, 0:1]
    own = raw - centre
    near_scale = 3.0 / jnp.full((1, rows), len_ref[0] * len_ref[0], F32)
    far_scale2 = 3.0 / jnp.full((1, rows), far_ref[0] * far_ref[0], F32)
    b_own[...] = right_side(own)
    a_near[1] = left_side(own, near_scale).T.astype(BF)
    at[...] = left_side(own, far_scale2, raw).T
    picks = []
    for o in range(STRIDE):
        part = at[pl.ds(o, rank, stride=STRIDE), :]
        a_far[o] = part.astype(BF)
        picks.append(part.T[72:80, :])

    loads[1].wait()
    offs = skel_ref[...] - STRIDE * lax.broadcasted_iota(jnp.int32, skel_ref.shape, 1)

    def choose(level, values):
        off = offs[level : level + 1, :]
        result = values[0]
        for o in range(1, STRIDE):
            result = jnp.where(off == o, values[o], result)
        return result

    for level in range(levels):
        psel[level, 0:3, :] = choose(level, picks)[0:3]

    loads[2].wait()
    r0 = r0_ref[...]
    hi, low = split2(r0)
    vec[1, 0:16, :] = hi
    vec[1, 16:32, :] = low
    marks = jnp.where(row_ids((16, rows)) == 0, 1.0, 0.0)
    vec[1, 32:48, :] = marks.astype(BF)

    def far_chunk(o, carry):
        left_part = a_far[o]
        for j in range(tiles):
            cols = pl.ds(j * tile, tile)
            fbuf[o, :, cols] = matern(dot(left_part, b_own[:, cols]), False).astype(BF)
        grp[o] = dot_t(vec[1], fbuf[o])
        return carry

    lax.fori_loop(0, STRIDE, far_chunk, 0)

    parts = [grp[o] for o in range(STRIDE)]
    sums = [g[0:16] + g[16:32] for g in parts]
    ones = [g[32:33] for g in parts]
    for level in order:
        cs1[level] = choose(level, sums)
        psel[level, 3:4, :] = choose(level, ones)

    pl.semaphore_wait(barrier, len(peers_a) + len(peers_b) + 2)

    sk, c1 = {}, {}
    for i, level in enumerate(order):
        peer = me + flip[level + 1]
        sk[level] = send(psel.at[level], prec.at[level], sk_send.at[level], sk_recv.at[level], peer)
        c1[level] = send(cs1.at[level], cr1.at[level], c1_send.at[level], c1_recv.at[level], peer)
        if i == min(1, levels - 1):
            nb = [
                send(pts_ref, nbp.at[0], nb_send.at[0], nb_recv.at[0], right),
                send(pts_ref, nbp.at[1], nb_send.at[1], nb_recv.at[1], left),
                send(r0_ref, nbr.at[0], nb_send.at[2], nb_recv.at[2], right),
                send(r0_ref, nbr.at[1], nb_send.at[3], nb_recv.at[3], left),
            ]

    acc_k[...] = jnp.zeros_like(acc_k)
    slope_ref[...] = jnp.zeros_like(slope_ref)

    def near_block(slot):
        def chunk(i, carry):
            at_rows = pl.ds(pl.multiple_of(i * tile, tile), tile)
            left_part = a_near[slot, at_rows, :]
            head = vec[slot, :, at_rows]
            for j in range(tiles):
                cols = pl.ds(j * tile, tile)
                value, slope = matern(dot(left_part, b_own[:, cols]), True)
                value = value.astype(BF)
                kbuf[slot, at_rows, cols] = value
                acc_k[:, cols] += dot(head, value)
                slope_ref[:, cols] += dot(head[0:16], slope.astype(BF))
            return carry

        lax.fori_loop(0, tiles, chunk, 0)

    def own_tiles(use):
        for i in range(tiles):
            for j in range(i, tiles):
                use(pl.ds(i * tile, tile), pl.ds(j * tile, tile), i == j)

    def own_near(rows_i, rows_j, diagonal):
        value, slope = matern(dot(a_near[1, rows_i, :], b_own[:, rows_j]), True)
        value, slope = value.astype(BF), slope.astype(BF)
        kbuf[1, rows_i, rows_j] = value
        head = vec[1, :, rows_i]
        acc_k[:, rows_j] += dot(head, value)
        slope_ref[:, rows_j] += dot(head[0:16], slope)
        if not diagonal:
            head = vec[1, :, rows_j]
            acc_k[:, rows_i] += dot_t(head, value)
            slope_ref[:, rows_i] += dot_t(head[0:16], slope)

    own_tiles(own_near)
    valid = [jnp.where(me > 0, 1.0, 0.0), jnp.where(me < n - 1, 1.0, 0.0)]
    for side, slot in ((0, 0), (1, 2)):
        nb[side].wait_recv()
        nb[2 + side].wait_recv()
        p8[0:3, :] = nbp[side]
        a_near[slot] = left_side(p8[...] - centre, near_scale).T.astype(BF)
        hi, low = split2(nbr[side] * valid[side])
        vec[slot, 0:16, :] = hi
        vec[slot, 16:32, :] = low
        vec[slot, 32:48, :] = (marks * valid[side]).astype(BF)
        near_block(slot)

    near_now = acc_k[...]
    sig, noise = sig_ref[0], noise_ref[0]
    rough = noise * r0 + sig * (near_now[0:16] + near_now[16:32] + near_now[32:33] * r0)
    first_a = start_reduce(0, pack([row_dot(r0, r0), row_dot(r0, rough)]))

    side_scale = far_scale2[:, 0:rank]

    def centred(four):
        full = jnp.concatenate([four, jnp.zeros_like(four)], axis=0)
        return jnp.where(row_ids(full.shape) < 3, full - centre, 0.0)

    arrivals = order[::-1]
    for start in range(0, levels, 4):
        batch = arrivals[start : start + 4]
        for level in batch:
            sk[level].wait_recv()
        for level in batch:
            a_side = left_side(centred(prec[level]), side_scale).T.astype(BF)
            b_side = right_side(centred(psel[level]))
            hi, low = split2(matern(dot(a_side, b_side), False))
            chi[level] = hi
            clo[level] = low

    def far_part(copies, received, with_ones):
        count = 24 if with_ones else 16
        sums = [jnp.zeros((count, rank), F32) for _ in range(STRIDE)]
        for level in reversed(order):
            copies[level].wait_recv()
            coef = received[level]
            if with_ones:
                tail = jnp.where(row_ids((8, rank)) == 0, prec[level, 3:4, :], 0.0)
                coef = jnp.concatenate([coef, tail], axis=0)
            hi, low = split2(coef)
            both = dot(jnp.concatenate([hi, low], axis=0), chi[level])
            mixed = both[:count] + both[count:] + dot(hi, clo[level])
            off = offs[level : level + 1, :]
            for o in range(STRIDE):
                sums[o] = sums[o] + jnp.where(off == o, mixed, 0.0)
        total = jnp.zeros((2 * count, rows), F32)
        for o in range(STRIDE):
            total = total + dot(jnp.concatenate(split2(sums[o]), axis=0), fbuf[o])
        return far_scale * (total[:count] + total[count:])

    far_now = far_part(c1, cr1, True)
    near_now = acc_k[...]
    row_sums = near_now[32:33] + far_now[16:17]
    image = noise * r0 + sig * (near_now[0:16] + near_now[16:32] + far_now[0:16] + row_sums * r0)
    slope_image = sig * slope_ref[...]
    slope_ref[...] = slope_image
    q_buf[...] = image
    rs_buf[...] = jnp.broadcast_to(row_sums, rs_buf.shape)
    hi, low = split2(image)
    qvec[1, 0:16, :] = hi
    qvec[1, 16:32, :] = low

    qs = [
        send(qvec.at[1], qvec.at[0], q_send.at[0], q_recv.at[0], right),
        send(qvec.at[1], qvec.at[2], q_send.at[1], q_recv.at[1], left),
    ]

    norm0, start_slope = row_dot(r0, r0), row_dot(r0, slope_image)

    parts = []
    for o in range(STRIDE):
        g = dot_t(qvec[1], fbuf[o])
        parts.append(g[0:16] + g[16:32])
    c2 = {}
    for level in order:
        cs2[level] = choose(level, parts)
        peer = me + flip[level + 1]
        c2[level] = send(cs2.at[level], cr2.at[level], c2_send.at[level], c2_recv.at[level], peer)

    acc_k[...] = jnp.zeros_like(acc_k)

    def own_again(rows_i, rows_j, diagonal):
        value = kbuf[1, rows_i, rows_j]
        acc_k[0:32, rows_j] += dot(qvec[1, :, rows_i], value)
        if not diagonal:
            acc_k[0:32, rows_i] += dot_t(qvec[1, :, rows_j], value)

    own_tiles(own_again)
    acc2 = acc_k[0:32, :]
    first_b = middle_reduce(0, first_a)
    for copy in nb + list(sk.values()) + list(c1.values()):
        copy.wait_send()
    for side, slot in ((0, 0), (1, 2)):
        qs[side].wait_recv()
        acc2 = acc2 + valid[side] * dot(qvec[slot], kbuf[slot])
    far_now = far_part(c2, cr2, False)
    image = q_buf[...]
    second = noise * image + sig * (acc2[0:16] + acc2[16:32] + far_now + rs_buf[0:1, :] * image)

    line = end_reduce(0, first_b)
    first_ref[...] = line
    step = unpack(line, 0) / unpack(line, 1)
    slope_image = slope_ref[...]
    r0 = r0_ref[...]
    r1 = r0 - step * image
    r1_image = image - step * second
    line = pack(
        [
            norm0,
            row_dot(r0, r1),
            row_dot(r1, r1),
            row_dot(r0, r1_image),
            row_dot(r1, r1_image),
            start_slope,
            row_dot(r1, slope_image),
        ]
    )
    second_a = start_reduce(1, line)
    r1_ref[...] = r1
    r1_image_ref[...] = r1_image
    for copy in qs + first_a + list(c2.values()) + first_b:
        copy.wait_send()
    second_b = middle_reduce(1, second_a)
    for copy in second_a:
        copy.wait_send()
    last_ref[...] = end_reduce(1, second_b)
    for copy in second_b:
        copy.wait_send()


def finish(scale, r1_ref, r1_image_ref, q_ref, slope_ref, first_ref, last_ref,
           sol_hbm, res_hbm, slope_hbm, trace_hbm, sol, res, trace_buf, sem):
    outs = [
        pltpu.make_async_copy(src, dst, sem.at[i])
        for i, (src, dst) in enumerate(
            ((slope_ref, slope_hbm), (sol, sol_hbm), (res, res_hbm), (trace_buf, trace_hbm))
        )
    ]
    outs[0].start()
    first, last = first_ref[...], last_ref[...]
    step = unpack(first, 0) / unpack(first, 1)
    norm0, along, square, image_along, image_own, start_slope, own_slope = [unpack(last, k) for k in range(7)]
    share = along / norm0
    gain = norm0 / (norm0 - along)
    inner0 = (norm0 - along) / step
    mixed = (along - square) / step + image_along
    norm1 = gain * gain * (square - share * along)
    inner1 = gain * gain * (image_own - share * mixed + share * share * inner0)
    cross1 = gain * (mixed - 2.0 * share * inner0)
    slope1 = gain * (own_slope - share * start_slope)
    alpha0 = step * gain
    beta = norm1 / norm0
    alpha1 = norm1 / (inner1 + beta * (cross1 + beta * inner0))
    q = q_ref[...]
    r0 = r1_ref[...] + step * q
    r1 = gain * (r1_ref[...] - share * r0)
    sol[...] = (alpha0 + alpha1 * beta) * r0 + alpha1 * r1
    outs[1].start()
    res[...] = r1 - alpha1 * (gain * (r1_image_ref[...] - share * q) + beta * q)
    outs[2].start()
    trace = (alpha0 * start_slope + alpha1 * (slope1 + beta * start_slope)) * scale
    trace_buf[...] = pack([trace])[:, 0:16]
    outs[3].start()
    for out in outs:
        out.wait()


def shards(points, right_sides, skeleton, lengthscale, far_length, signal, noise_var):
    n = lax.axis_size("loc")
    bits = n.bit_length() - 1
    rows = points.shape[1]
    levels, rank = skeleton.shape
    split = min(5, bits // 2 + 1)
    groups = (tuple(range(split)), tuple(range(split, bits)))
    size_a, size_b = 2 ** len(groups[0]), 2 ** len(groups[1])
    vmem = pl.BlockSpec(memory_space=pltpu.VMEM)
    smem = pl.BlockSpec(memory_space=pltpu.SMEM)
    dma = pltpu.SemaphoreType.DMA
    hbm = pl.BlockSpec(memory_space=pltpu.HBM)
    scratch = [
        pltpu.VMEM((3, rows), F32),
        pltpu.VMEM((16, rows), F32),
        pltpu.VMEM((levels, rank), jnp.int32),
        dma((3,)),
        pltpu.VMEM((8, rows), F32),
        pltpu.VMEM((3, VROWS, rows), BF),
        pltpu.VMEM((3, 32, rows), BF),
        pltpu.VMEM((2, 3, rows), F32),
        pltpu.VMEM((2, 16, rows), F32),
        pltpu.VMEM((rows, LANES), F32),
        pltpu.VMEM((3, rows, LANES), BF),
        pltpu.VMEM((STRIDE, rank, LANES), BF),
        pltpu.VMEM((LANES, rows), BF),
        pltpu.VMEM((3, rows, rows), BF),
        pltpu.VMEM((STRIDE, rank, rows), BF),
        pltpu.VMEM((levels, 4, rank), F32),
        pltpu.VMEM((levels, 4, rank), F32),
        pltpu.VMEM((levels, rank, rank), BF),
        pltpu.VMEM((levels, rank, rank), BF),
        pltpu.VMEM((STRIDE, VROWS, rank), F32),
        pltpu.VMEM((levels, 16, rank), F32),
        pltpu.VMEM((levels, 16, rank), F32),
        pltpu.VMEM((levels, 16, rank), F32),
        pltpu.VMEM((levels, 16, rank), F32),
        pltpu.VMEM((VROWS, rows), F32),
        pltpu.VMEM((8, rows), F32),
        pltpu.VMEM((2, size_a, 1, LANES), F32),
        pltpu.VMEM((2, size_b, 1, LANES), F32),
        dma((4,)), dma((4,)), dma((2,)), dma((2,)),
        dma((levels,)), dma((levels,)), dma((levels,)), dma((levels,)), dma((levels,)), dma((levels,)),
        dma((2, size_a - 1)), dma((2, size_a - 1)), dma((2, size_b - 1)), dma((2, size_b - 1)),
    ]
    block = jax.ShapeDtypeStruct(right_sides.shape, F32)
    row = jax.ShapeDtypeStruct((1, LANES), F32)
    parts = pl.pallas_call(
        functools.partial(kernel, bits, groups),
        out_shape=(block,) * 4 + (row,) * 2,
        in_specs=[hbm] * 3 + [smem] * 4,
        out_specs=(vmem,) * 6,
        scratch_shapes=scratch,
        compiler_params=pltpu.CompilerParams(collective_id=0, has_side_effects=True, vmem_limit_bytes=56_200_000),
        name="cg",
    )(points, right_sides, skeleton, lengthscale, far_length, signal, noise_var)
    probes = right_sides.shape[0]
    outs = pl.pallas_call(
        functools.partial(finish, 1.0 / (n * rows)),
        out_shape=(block, block, block, jax.ShapeDtypeStruct((1, probes), F32)),
        in_specs=[vmem] * 6,
        out_specs=(hbm,) * 4,
        scratch_shapes=[
            pltpu.VMEM(right_sides.shape, F32), pltpu.VMEM(right_sides.shape, F32), pltpu.VMEM((1, probes), F32), dma((4,)),
        ],
        compiler_params=pltpu.CompilerParams(vmem_limit_bytes=2 * 2**20),
        name="finish",
    )(*parts)
    return outs[0], outs[1], outs[2], outs[3].reshape(probes)


def solution(mesh):
    placed = (P(None, "loc"), P(None, "loc"), P(None, "loc"), P(), P(), P(), P())
    return jax.shard_map(
        shards,
        mesh=mesh,
        in_specs=placed,
        out_specs=(P(None, "loc"), P(None, "loc"), P(None, "loc"), P()),
        check_vma=False,
    )
```

```python
import functools

import jax
import jax.numpy as jnp
from jax import lax
from jax.experimental import pallas as pl
from jax.experimental.pallas import tpu as pltpu
from jax.sharding import PartitionSpec as P

F32 = jnp.float32
BF = jnp.bfloat16
LOG2E = 1.4426950408889634
STRIDE = 4
LANES = 128
VROWS = 48
MESH = pl.DeviceIdType.MESH


def split2(x):
    hi = x.astype(BF)
    return hi, (x - hi.astype(F32)).astype(BF)


def split3(x):
    hi = x.astype(BF).astype(F32)
    rest = x - hi
    mid = rest.astype(BF).astype(F32)
    return hi, mid, rest - mid


def row_ids(shape):
    return lax.broadcasted_iota(jnp.int32, shape, 0)


def left_side(pts, scale, extra=None):
    rows = row_ids(pts.shape)
    square = scale * jnp.sum(pts * pts, axis=0, keepdims=True)
    full = jnp.where(rows < 3, -2.0 * scale * pts, jnp.where(rows == 3, square, jnp.where(rows == 4, scale, 0.0)))
    hi, mid, low = split3(full)
    parts = [hi, hi, hi, mid, mid, mid, low, low, low]
    if extra is not None:
        parts.append(extra)
    filler = jnp.zeros((LANES - 8 * len(parts), pts.shape[1]), F32)
    return jnp.concatenate(parts + [filler], axis=0)


def right_side(pts):
    rows = row_ids(pts.shape)
    square = jnp.sum(pts * pts, axis=0, keepdims=True)
    full = jnp.where(rows < 3, pts, jnp.where(rows == 3, 1.0, jnp.where(rows == 4, square, 0.0)))
    hi, mid, low = split3(full)
    filler = jnp.zeros((LANES - 72, pts.shape[1]), F32)
    return jnp.concatenate([hi, mid, low] * 3 + [filler], axis=0).astype(BF)


def matern(square, want_slope):
    square = jnp.maximum(square, 1e-30)
    scaled = square * lax.rsqrt(square)
    decay = jnp.exp2(scaled * (-LOG2E))
    first = scaled * decay
    if want_slope:
        return decay + first, scaled * first
    return decay + first


def dot(a, b):
    return jnp.dot(a, b, preferred_element_type=F32)


def dot_t(a, b):
    return lax.dot_general(a, b, (((1,), (1,)), ((), ())), preferred_element_type=F32)


def pack(columns):
    lanes = lax.broadcasted_iota(jnp.int32, (16, LANES), 1)
    rows = row_ids((16, LANES))
    total = jnp.zeros((16, LANES), F32)
    for k, column in enumerate(columns):
        total = jnp.where(lanes == rows + 16 * k, column, total)
    return jnp.sum(total, axis=0, keepdims=True)


def unpack(line, k):
    lanes = lax.broadcasted_iota(jnp.int32, (16, LANES), 1)
    rows = row_ids((16, LANES))
    return jnp.sum(jnp.where(lanes == rows + 16 * k, line, 0.0), axis=1, keepdims=True)


def row_dot(a, b):
    return jnp.sum(a * b, axis=1, keepdims=True)


def kernel(
    bits, groups, pts_hbm, r0_hbm, skel_hbm, len_ref, far_ref, sig_ref, noise_ref,
    r1_ref, r1_image_ref, q_buf, slope_ref, first_ref, last_ref,
    pts_ref, r0_ref, skel_ref, in_sem, p8, vec, qvec, nbp, nbr, at, a_near, a_far, b_own, kbuf, fbuf, psel, prec, chi, clo, grp,
    cs1, cr1, cs2, cr2, acc_k, rs_buf, red_a, red_b,
    nb_send, nb_recv, q_send, q_recv, sk_send, sk_recv, c1_send, c1_recv, c2_send, c2_recv,
    ra_send, ra_recv, rb_send, rb_recv,
):
    n = 2**bits
    levels, rank = skel_ref.shape
    rows = pts_ref.shape[1]
    tile = rank
    tiles = rows // tile
    far_scale = 1.0 / (rank * rank * levels)
    loads = [
        pltpu.make_async_copy(src, dst, in_sem.at[i])
        for i, (src, dst) in enumerate(((pts_hbm, pts_ref), (skel_hbm, skel_ref), (r0_hbm, r0_ref)))
    ]
    for load in loads:
        load.start()
    me = lax.axis_index("loc")
    flip = [2**b * (1 - 2 * ((me // 2**b) % 2)) for b in range(bits)]
    right = (me + 1) % n
    left = (me + n - 1) % n
    group_a, group_b = groups

    def peers(group):
        found = []
        for d in range(1, 2 ** len(group)):
            found.append(me + sum(flip[b] for i, b in enumerate(group) if (d >> i) & 1))
        return found

    peers_a, peers_b = peers(group_a), peers(group_b)
    barrier = pltpu.get_barrier_semaphore()
    for peer in peers_a[::-1] + peers_b + [left, right]:
        pl.semaphore_signal(barrier, inc=1, device_id=(peer,), device_id_type=MESH)

    def send(src, dst, ssem, rsem, peer):
        copy = pltpu.make_async_remote_copy(
            src_ref=src, dst_ref=dst, send_sem=ssem, recv_sem=rsem, device_id=(peer,), device_id_type=MESH
        )
        copy.start()
        return copy

    def start_reduce(step, line):
        red_a[step, 0] = line
        return [
            send(red_a.at[step, 0], red_a.at[step, d + 1], ra_send.at[step, d], ra_recv.at[step, d], peer)
            for d, peer in enumerate(peers_a)
        ]

    def halve(values):
        while values.shape[0] > 1:
            half = values.shape[0] // 2
            values = values[:half] + values[half:]
        return values[0]

    def middle_reduce(step, copies):
        for copy in copies:
            copy.wait_recv()
        red_b[step, 0] = halve(red_a[step])
        return [
            send(red_b.at[step, 0], red_b.at[step, d + 1], rb_send.at[step, d], rb_recv.at[step, d], peer)
            for d, peer in enumerate(peers_b)
        ]

    def end_reduce(step, copies):
        for copy in copies:
            copy.wait_recv()
        return halve(red_b[step])

    order = sorted(range(levels), key=lambda level: -(2**level if level < 4 else 2 ** (level % 2)))

    p8[...] = jnp.zeros_like(p8)
    loads[0].wait()
    p8[0:3, :] = pts_ref[...]
    raw = p8[...]
    centre = raw[:, 0:1]
    own = raw - centre
    near_scale = 3.0 / jnp.full((1, rows), len_ref[0] * len_ref[0], F32)
    far_scale2 = 3.0 / jnp.full((1, rows), far_ref[0] * far_ref[0], F32)
    b_own[...] = right_side(own)
    at[...] = left_side(own, far_scale2, raw).T
    picks = []
    for o in range(STRIDE):
        part = at[pl.ds(o, rank, stride=STRIDE), :]
        a_far[o] = part.astype(BF)
        picks.append(part.T[72:80, :])

    loads[1].wait()
    offs = skel_ref[...] - STRIDE * lax.broadcasted_iota(jnp.int32, skel_ref.shape, 1)

    def choose(level, values):
        off = offs[level : level + 1, :]
        result = values[0]
        for o in range(1, STRIDE):
            result = jnp.where(off == o, values[o], result)
        return result

    for level in range(levels):
        psel[level, 0:3, :] = choose(level, picks)[0:3]

    loads[2].wait()
    r0 = r0_ref[...]
    hi, low = split2(r0)
    vec[1, 0:16, :] = hi
    vec[1, 16:32, :] = low
    marks = jnp.where(row_ids((16, rows)) == 0, 1.0, 0.0)
    vec[1, 32:48, :] = marks.astype(BF)

    def far_chunk(o, carry):
        left_part = a_far[o]
        for j in range(tiles):
            cols = pl.ds(j * tile, tile)
            fbuf[o, :, cols] = matern(dot(left_part, b_own[:, cols]), False).astype(BF)
        grp[o] = dot_t(vec[1], fbuf[o])
        return carry

    lax.fori_loop(0, STRIDE, far_chunk, 0)

    parts = [grp[o] for o in range(STRIDE)]
    sums = [g[0:16] + g[16:32] for g in parts]
    ones = [g[32:33] for g in parts]
    for level in order:
        cs1[level] = choose(level, sums)
        psel[level, 3:4, :] = choose(level, ones)

    pl.semaphore_wait(barrier, len(peers_a) + len(peers_b) + 2)

    sk, c1 = {}, {}
    for i, level in enumerate(order):
        peer = me + flip[level + 1]
        sk[level] = send(psel.at[level], prec.at[level], sk_send.at[level], sk_recv.at[level], peer)
        c1[level] = send(cs1.at[level], cr1.at[level], c1_send.at[level], c1_recv.at[level], peer)
        if i == min(1, levels - 1):
            nb = [
                send(pts_ref, nbp.at[0], nb_send.at[0], nb_recv.at[0], right),
                send(pts_ref, nbp.at[1], nb_send.at[1], nb_recv.at[1], left),
                send(r0_ref, nbr.at[0], nb_send.at[2], nb_recv.at[2], right),
                send(r0_ref, nbr.at[1], nb_send.at[3], nb_recv.at[3], left),
            ]

    acc_k[...] = jnp.zeros_like(acc_k)
    slope_ref[...] = jnp.zeros_like(slope_ref)

    def near_block(slot):
        def chunk(i, carry):
            at_rows = pl.ds(pl.multiple_of(i * tile, tile), tile)
            left_part = a_near[slot, at_rows, :]
            head = vec[slot, :, at_rows]
            for j in range(tiles):
                cols = pl.ds(j * tile, tile)
                value, slope = matern(dot(left_part, b_own[:, cols]), True)
                value = value.astype(BF)
                kbuf[slot, at_rows, cols] = value
                acc_k[:, cols] += dot(head, value)
                slope_ref[:, cols] += dot(head[0:16], slope.astype(BF))
            return carry

        lax.fori_loop(0, tiles, chunk, 0)

    def own_tiles(use):
        for i in range(tiles):
            for j in range(i, tiles):
                use(pl.ds(i * tile, tile), pl.ds(j * tile, tile), i == j)

    def own_near(rows_i, rows_j, diagonal):
        value, slope = matern(dot(a_near[1, rows_i, :], b_own[:, rows_j]), True)
        value, slope = value.astype(BF), slope.astype(BF)
        kbuf[1, rows_i, rows_j] = value
        head = vec[1, :, rows_i]
        acc_k[:, rows_j] += dot(head, value)
        slope_ref[:, rows_j] += dot(head[0:16], slope)
        if not diagonal:
            head = vec[1, :, rows_j]
            acc_k[:, rows_i] += dot_t(head, value)
            slope_ref[:, rows_i] += dot_t(head[0:16], slope)

    a_near[1] = left_side(own, near_scale).T.astype(BF)
    own_tiles(own_near)
    valid = [jnp.where(me > 0, 1.0, 0.0), jnp.where(me < n - 1, 1.0, 0.0)]
    for side, slot in ((0, 0), (1, 2)):
        nb[side].wait_recv()
        nb[2 + side].wait_recv()
        p8[0:3, :] = nbp[side]
        a_near[slot] = left_side(p8[...] - centre, near_scale).T.astype(BF)
        hi, low = split2(nbr[side] * valid[side])
        vec[slot, 0:16, :] = hi
        vec[slot, 16:32, :] = low
        vec[slot, 32:48, :] = (marks * valid[side]).astype(BF)
        near_block(slot)

    near_now = acc_k[...]
    sig, noise = sig_ref[0], noise_ref[0]
    rough = noise * r0 + sig * (near_now[0:16] + near_now[16:32] + near_now[32:33] * r0)
    first_a = start_reduce(0, pack([row_dot(r0, r0), row_dot(r0, rough)]))

    side_scale = far_scale2[:, 0:rank]

    def centred(four):
        full = jnp.concatenate([four, jnp.zeros_like(four)], axis=0)
        return jnp.where(row_ids(full.shape) < 3, full - centre, 0.0)

    arrivals = order[::-1]
    for start in range(0, levels, 4):
        batch = arrivals[start : start + 4]
        for level in batch:
            sk[level].wait_recv()
        for level in batch:
            a_side = left_side(centred(prec[level]), side_scale).T.astype(BF)
            b_side = right_side(centred(psel[level]))
            hi, low = split2(matern(dot(a_side, b_side), False))
            chi[level] = hi
            clo[level] = low

    def far_part(copies, received, with_ones):
        count = 24 if with_ones else 16
        sums = [jnp.zeros((count, rank), F32) for _ in range(STRIDE)]
        for level in reversed(order):
            copies[level].wait_recv()
            coef = received[level]
            if with_ones:
                tail = jnp.where(row_ids((8, rank)) == 0, prec[level, 3:4, :], 0.0)
                coef = jnp.concatenate([coef, tail], axis=0)
            hi, low = split2(coef)
            both = dot(jnp.concatenate([hi, low], axis=0), chi[level])
            mixed = both[:count] + both[count:] + dot(hi, clo[level])
            off = offs[level : level + 1, :]
            for o in range(STRIDE):
                sums[o] = sums[o] + jnp.where(off == o, mixed, 0.0)
        halves = [jnp.concatenate(split2(part), axis=0) for part in sums]
        total = dot(jnp.concatenate(halves, axis=1), fbuf[...].reshape(rows, rows))
        return far_scale * (total[:count] + total[count:])

    far_now = far_part(c1, cr1, True)
    near_now = acc_k[...]
    row_sums = near_now[32:33] + far_now[16:17]
    image = noise * r0 + sig * (near_now[0:16] + near_now[16:32] + far_now[0:16] + row_sums * r0)
    slope_image = sig * slope_ref[...]
    slope_ref[...] = slope_image
    q_buf[...] = image
    rs_buf[...] = jnp.broadcast_to(row_sums, rs_buf.shape)
    hi, low = split2(image)
    qvec[1, 0:16, :] = hi
    qvec[1, 16:32, :] = low

    qs = [
        send(qvec.at[1], qvec.at[0], q_send.at[0], q_recv.at[0], right),
        send(qvec.at[1], qvec.at[2], q_send.at[1], q_recv.at[1], left),
    ]

    norm0, start_slope = row_dot(r0, r0), row_dot(r0, slope_image)

    parts = []
    both = dot_t(qvec[1], fbuf[...].reshape(rows, rows))
    for o in range(STRIDE):
        g = both[:, o * rank : (o + 1) * rank]
        parts.append(g[0:16] + g[16:32])
    c2 = {}
    for level in order:
        cs2[level] = choose(level, parts)
        peer = me + flip[level + 1]
        c2[level] = send(cs2.at[level], cr2.at[level], c2_send.at[level], c2_recv.at[level], peer)

    acc_k[...] = jnp.zeros_like(acc_k)

    def own_again(rows_i, rows_j, diagonal):
        value = kbuf[1, rows_i, rows_j]
        acc_k[0:32, rows_j] += dot(qvec[1, :, rows_i], value)
        if not diagonal:
            acc_k[0:32, rows_i] += dot_t(qvec[1, :, rows_j], value)

    own_tiles(own_again)
    acc2 = acc_k[0:32, :]
    first_b = middle_reduce(0, first_a)
    for copy in nb + list(sk.values()) + list(c1.values()):
        copy.wait_send()
    for side, slot in ((0, 0), (1, 2)):
        qs[side].wait_recv()
        acc2 = acc2 + valid[side] * dot(qvec[slot], kbuf[slot])
    far_now = far_part(c2, cr2, False)
    image = q_buf[...]
    second = noise * image + sig * (acc2[0:16] + acc2[16:32] + far_now + rs_buf[0:1, :] * image)

    line = end_reduce(0, first_b)
    first_ref[...] = line
    step = unpack(line, 0) / unpack(line, 1)
    slope_image = slope_ref[...]
    r0 = r0_ref[...]
    r1 = r0 - step * image
    r1_image = image - step * second
    line = pack(
        [
            norm0,
            row_dot(r0, r1),
            row_dot(r1, r1),
            row_dot(r0, r1_image),
            row_dot(r1, r1_image),
            start_slope,
            row_dot(r1, slope_image),
        ]
    )
    second_a = start_reduce(1, line)
    r1_ref[...] = r1
    r1_image_ref[...] = r1_image
    for copy in qs + first_a + list(c2.values()) + first_b:
        copy.wait_send()
    second_b = middle_reduce(1, second_a)
    for copy in second_a:
        copy.wait_send()
    last_ref[...] = end_reduce(1, second_b)
    for copy in second_b:
        copy.wait_send()


def finish(scale, r1_ref, r1_image_ref, q_ref, slope_ref, first_ref, last_ref,
           sol_hbm, res_hbm, slope_hbm, trace_hbm, sol, res, trace_buf, sem):
    outs = [
        pltpu.make_async_copy(src, dst, sem.at[i])
        for i, (src, dst) in enumerate(
            ((slope_ref, slope_hbm), (sol, sol_hbm), (res, res_hbm), (trace_buf, trace_hbm))
        )
    ]
    outs[0].start()
    first, last = first_ref[...], last_ref[...]
    step = unpack(first, 0) / unpack(first, 1)
    norm0, along, square, image_along, image_own, start_slope, own_slope = [unpack(last, k) for k in range(7)]
    share = along / norm0
    gain = norm0 / (norm0 - along)
    inner0 = (norm0 - along) / step
    mixed = (along - square) / step + image_along
    norm1 = gain * gain * (square - share * along)
    inner1 = gain * gain * (image_own - share * mixed + share * share * inner0)
    cross1 = gain * (mixed - 2.0 * share * inner0)
    slope1 = gain * (own_slope - share * start_slope)
    alpha0 = step * gain
    beta = norm1 / norm0
    alpha1 = norm1 / (inner1 + beta * (cross1 + beta * inner0))
    q = q_ref[...]
    r0 = r1_ref[...] + step * q
    r1 = gain * (r1_ref[...] - share * r0)
    sol[...] = (alpha0 + alpha1 * beta) * r0 + alpha1 * r1
    outs[1].start()
    res[...] = r1 - alpha1 * (gain * (r1_image_ref[...] - share * q) + beta * q)
    outs[2].start()
    trace = (alpha0 * start_slope + alpha1 * (slope1 + beta * start_slope)) * scale
    trace_buf[...] = pack([trace])[:, 0:16]
    outs[3].start()
    for out in outs:
        out.wait()


def shards(points, right_sides, skeleton, lengthscale, far_length, signal, noise_var):
    n = lax.axis_size("loc")
    bits = n.bit_length() - 1
    rows = points.shape[1]
    levels, rank = skeleton.shape
    split = min(5, bits // 2 + 1)
    groups = (tuple(range(split)), tuple(range(split, bits)))
    size_a, size_b = 2 ** len(groups[0]), 2 ** len(groups[1])
    vmem = pl.BlockSpec(memory_space=pltpu.VMEM)
    smem = pl.BlockSpec(memory_space=pltpu.SMEM)
    dma = pltpu.SemaphoreType.DMA
    hbm = pl.BlockSpec(memory_space=pltpu.HBM)
    scratch = [
        pltpu.VMEM((3, rows), F32),
        pltpu.VMEM((16, rows), F32),
        pltpu.VMEM((levels, rank), jnp.int32),
        dma((3,)),
        pltpu.VMEM((8, rows), F32),
        pltpu.VMEM((3, VROWS, rows), BF),
        pltpu.VMEM((3, 32, rows), BF),
        pltpu.VMEM((2, 3, rows), F32),
        pltpu.VMEM((2, 16, rows), F32),
        pltpu.VMEM((rows, LANES), F32),
        pltpu.VMEM((3, rows, LANES), BF),
        pltpu.VMEM((STRIDE, rank, LANES), BF),
        pltpu.VMEM((LANES, rows), BF),
        pltpu.VMEM((3, rows, rows), BF),
        pltpu.VMEM((STRIDE, rank, rows), BF),
        pltpu.VMEM((levels, 4, rank), F32),
        pltpu.VMEM((levels, 4, rank), F32),
        pltpu.VMEM((levels, rank, rank), BF),
        pltpu.VMEM((levels, rank, rank), BF),
        pltpu.VMEM((STRIDE, VROWS, rank), F32),
        pltpu.VMEM((levels, 16, rank), F32),
        pltpu.VMEM((levels, 16, rank), F32),
        pltpu.VMEM((levels, 16, rank), F32),
        pltpu.VMEM((levels, 16, rank), F32),
        pltpu.VMEM((VROWS, rows), F32),
        pltpu.VMEM((8, rows), F32),
        pltpu.VMEM((2, size_a, 1, LANES), F32),
        pltpu.VMEM((2, size_b, 1, LANES), F32),
        dma((4,)), dma((4,)), dma((2,)), dma((2,)),
        dma((levels,)), dma((levels,)), dma((levels,)), dma((levels,)), dma((levels,)), dma((levels,)),
        dma((2, size_a - 1)), dma((2, size_a - 1)), dma((2, size_b - 1)), dma((2, size_b - 1)),
    ]
    block = jax.ShapeDtypeStruct(right_sides.shape, F32)
    row = jax.ShapeDtypeStruct((1, LANES), F32)
    parts = pl.pallas_call(
        functools.partial(kernel, bits, groups),
        out_shape=(block,) * 4 + (row,) * 2,
        in_specs=[hbm] * 3 + [smem] * 4,
        out_specs=(vmem,) * 6,
        scratch_shapes=scratch,
        compiler_params=pltpu.CompilerParams(collective_id=0, has_side_effects=True, vmem_limit_bytes=56_200_000),
        name="cg",
    )(*[pltpu.with_memory_space_constraint(a, pltpu.HBM) for a in (points, right_sides, skeleton)], lengthscale, far_length, signal, noise_var)
    probes = right_sides.shape[0]
    outs = pl.pallas_call(
        functools.partial(finish, 1.0 / (n * rows)),
        out_shape=(block, block, block, jax.ShapeDtypeStruct((1, probes), F32)),
        in_specs=[vmem] * 6,
        out_specs=(hbm,) * 4,
        scratch_shapes=[
            pltpu.VMEM(right_sides.shape, F32), pltpu.VMEM(right_sides.shape, F32), pltpu.VMEM((1, probes), F32), dma((4,)),
        ],
        compiler_params=pltpu.CompilerParams(vmem_limit_bytes=2 * 2**20),
        name="finish",
    )(*parts)
    return outs[0], outs[1], outs[2], outs[3].reshape(probes)


def solution(mesh):
    placed = (P(None, "loc"), P(None, "loc"), P(None, "loc"), P(), P(), P(), P())
    return jax.shard_map(
        shards,
        mesh=mesh,
        in_specs=placed,
        out_specs=(P(None, "loc"), P(None, "loc"), P(None, "loc"), P()),
        check_vma=False,
    )
```

```python
import functools

import jax
import jax.numpy as jnp
from jax import lax
from jax.experimental import pallas as pl
from jax.experimental.pallas import tpu as pltpu
from jax.sharding import PartitionSpec as P

F32 = jnp.float32
BF = jnp.bfloat16
LOG2E = 1.4426950408889634
STRIDE = 4
LANES = 128
VROWS = 48
MESH = pl.DeviceIdType.MESH


def split2(x):
    hi = x.astype(BF)
    return hi, (x - hi.astype(F32)).astype(BF)


def split3(x):
    hi = x.astype(BF).astype(F32)
    rest = x - hi
    mid = rest.astype(BF).astype(F32)
    return hi, mid, rest - mid


def row_ids(shape):
    return lax.broadcasted_iota(jnp.int32, shape, 0)


def left_side(pts, scale, extra=None):
    rows = row_ids(pts.shape)
    square = scale * jnp.sum(pts * pts, axis=0, keepdims=True)
    full = jnp.where(rows < 3, -2.0 * scale * pts, jnp.where(rows == 3, square, jnp.where(rows == 4, scale, 0.0)))
    hi, mid, low = split3(full)
    parts = [hi, hi, hi, mid, mid, mid, low, low, low]
    if extra is not None:
        parts.append(extra)
    filler = jnp.zeros((LANES - 8 * len(parts), pts.shape[1]), F32)
    return jnp.concatenate(parts + [filler], axis=0)


def right_side(pts):
    rows = row_ids(pts.shape)
    square = jnp.sum(pts * pts, axis=0, keepdims=True)
    full = jnp.where(rows < 3, pts, jnp.where(rows == 3, 1.0, jnp.where(rows == 4, square, 0.0)))
    hi, mid, low = split3(full)
    filler = jnp.zeros((LANES - 72, pts.shape[1]), F32)
    return jnp.concatenate([hi, mid, low] * 3 + [filler], axis=0).astype(BF)


def matern(square, want_slope):
    square = jnp.maximum(square, 1e-30)
    scaled = square * lax.rsqrt(square)
    decay = jnp.exp2(scaled * (-LOG2E))
    first = scaled * decay
    if want_slope:
        return decay + first, scaled * first
    return decay + first


def dot(a, b):
    return jnp.dot(a, b, preferred_element_type=F32)


def dot_t(a, b):
    return lax.dot_general(a, b, (((1,), (1,)), ((), ())), preferred_element_type=F32)


def pack(columns):
    lanes = lax.broadcasted_iota(jnp.int32, (16, LANES), 1)
    rows = row_ids((16, LANES))
    total = jnp.zeros((16, LANES), F32)
    for k, column in enumerate(columns):
        total = jnp.where(lanes == rows + 16 * k, column, total)
    return jnp.sum(total, axis=0, keepdims=True)


def unpack(line, k):
    lanes = lax.broadcasted_iota(jnp.int32, (16, LANES), 1)
    rows = row_ids((16, LANES))
    return jnp.sum(jnp.where(lanes == rows + 16 * k, line, 0.0), axis=1, keepdims=True)


def row_dot(a, b):
    return jnp.sum(a * b, axis=1, keepdims=True)


def kernel(
    bits, groups, pts_hbm, r0_hbm, skel_hbm, len_ref, far_ref, sig_ref, noise_ref,
    r1_ref, r1_image_ref, q_buf, slope_ref, first_ref, last_ref,
    pts_ref, r0_ref, skel_ref, in_sem, p8, vec, qvec, nbp, nbr, at, a_near, a_far, b_own, kbuf, fbuf, psel, prec, chi, clo, grp,
    cs1, cr1, cs2, cr2, acc_k, rs_buf, basis, red_a, red_b,
    nb_send, nb_recv, q_send, q_recv, sk_send, sk_recv, c1_send, c1_recv, c2_send, c2_recv,
    ra_send, ra_recv, rb_send, rb_recv,
):
    n = 2**bits
    levels, rank = skel_ref.shape
    rows = pts_ref.shape[1]
    tile = rank
    tiles = rows // tile
    far_scale = 1.0 / (rank * rank * levels)
    loads = [
        pltpu.make_async_copy(src, dst, in_sem.at[i])
        for i, (src, dst) in enumerate(((pts_hbm, pts_ref), (skel_hbm, skel_ref), (r0_hbm, r0_ref)))
    ]
    for load in loads:
        load.start()
    me = lax.axis_index("loc")
    flip = [2**b * (1 - 2 * ((me // 2**b) % 2)) for b in range(bits)]
    right = (me + 1) % n
    left = (me + n - 1) % n
    group_a, group_b = groups

    def peers(group):
        found = []
        for d in range(1, 2 ** len(group)):
            found.append(me + sum(flip[b] for i, b in enumerate(group) if (d >> i) & 1))
        return found

    peers_a, peers_b = peers(group_a), peers(group_b)
    barrier = pltpu.get_barrier_semaphore()
    for peer in peers_a[::-1] + peers_b + [left, right]:
        pl.semaphore_signal(barrier, inc=1, device_id=(peer,), device_id_type=MESH)

    def send(src, dst, ssem, rsem, peer):
        copy = pltpu.make_async_remote_copy(
            src_ref=src, dst_ref=dst, send_sem=ssem, recv_sem=rsem, device_id=(peer,), device_id_type=MESH
        )
        copy.start()
        return copy

    def start_reduce(step, line):
        red_a[step, 0] = line
        return [
            send(red_a.at[step, 0], red_a.at[step, d + 1], ra_send.at[step, d], ra_recv.at[step, d], peer)
            for d, peer in enumerate(peers_a)
        ]

    def halve(values):
        while values.shape[0] > 1:
            half = values.shape[0] // 2
            values = values[:half] + values[half:]
        return values[0]

    def middle_reduce(step, copies):
        for copy in copies:
            copy.wait_recv()
        red_b[step, 0] = halve(red_a[step])
        return [
            send(red_b.at[step, 0], red_b.at[step, d + 1], rb_send.at[step, d], rb_recv.at[step, d], peer)
            for d, peer in enumerate(peers_b)
        ]

    def end_reduce(step, copies):
        for copy in copies:
            copy.wait_recv()
        return halve(red_b[step])

    order = sorted(range(levels), key=lambda level: -(2**level if level < 4 else 2 ** (level % 2)))

    p8[...] = jnp.zeros_like(p8)
    loads[0].wait()
    p8[0:3, :] = pts_ref[...]
    raw = p8[...]
    centre = raw[:, 0:1]
    own = raw - centre
    near_scale = 3.0 / jnp.full((1, rows), len_ref[0] * len_ref[0], F32)
    far_scale2 = 3.0 / jnp.full((1, rows), far_ref[0] * far_ref[0], F32)
    b_own[...] = right_side(own)
    at[...] = left_side(own, far_scale2, raw).T
    picks = []
    for o in range(STRIDE):
        part = at[pl.ds(o, rank, stride=STRIDE), :]
        a_far[o] = part.astype(BF)
        picks.append(part.T[72:80, :])

    loads[1].wait()
    offs = skel_ref[...] - STRIDE * lax.broadcasted_iota(jnp.int32, skel_ref.shape, 1)

    def choose(level, values):
        off = offs[level : level + 1, :]
        result = values[0]
        for o in range(1, STRIDE):
            result = jnp.where(off == o, values[o], result)
        return result

    for level in range(levels):
        psel[level, 0:3, :] = choose(level, picks)[0:3]

    loads[2].wait()
    r0 = r0_ref[...]
    hi, low = split2(r0)
    vec[1, 0:16, :] = hi
    vec[1, 16:32, :] = low
    marks = jnp.where(row_ids((16, rows)) == 0, 1.0, 0.0)
    vec[1, 32:48, :] = marks.astype(BF)

    def far_chunk(o, carry):
        left_part = a_far[o]
        for j in range(tiles):
            cols = pl.ds(j * tile, tile)
            fbuf[o, :, cols] = matern(dot(left_part, b_own[:, cols]), False).astype(BF)
        grp[o] = dot_t(vec[1], fbuf[o])
        return carry

    lax.fori_loop(0, STRIDE, far_chunk, 0)

    parts = [grp[o] for o in range(STRIDE)]
    sums = [g[0:16] + g[16:32] for g in parts]
    ones = [g[32:33] for g in parts]
    for level in order:
        cs1[level] = choose(level, sums)
        psel[level, 3:4, :] = choose(level, ones)

    pl.semaphore_wait(barrier, len(peers_a) + len(peers_b) + 2)

    sk, c1 = {}, {}

    def send_coefs(level):
        peer = me + flip[level + 1]
        c1[level] = send(cs1.at[level], cr1.at[level], c1_send.at[level], c1_recv.at[level], peer)

    for i, level in enumerate(order):
        if i < 2:
            send_coefs(level)
        peer = me + flip[level + 1]
        sk[level] = send(psel.at[level], prec.at[level], sk_send.at[level], sk_recv.at[level], peer)
    nb = [
        send(pts_ref, nbp.at[0], nb_send.at[0], nb_recv.at[0], right),
        send(pts_ref, nbp.at[1], nb_send.at[1], nb_recv.at[1], left),
        send(r0_ref, nbr.at[0], nb_send.at[2], nb_recv.at[2], right),
        send(r0_ref, nbr.at[1], nb_send.at[3], nb_recv.at[3], left),
    ]
    for level in order[2:]:
        send_coefs(level)

    acc_k[...] = jnp.zeros_like(acc_k)
    slope_ref[...] = jnp.zeros_like(slope_ref)

    def near_block(slot):
        def chunk(i, carry):
            at_rows = pl.ds(pl.multiple_of(i * tile, tile), tile)
            left_part = a_near[slot, at_rows, :]
            head = vec[slot, :, at_rows]
            for j in range(tiles):
                cols = pl.ds(j * tile, tile)
                value, slope = matern(dot(left_part, b_own[:, cols]), True)
                value = value.astype(BF)
                kbuf[slot, at_rows, cols] = value
                acc_k[:, cols] += dot(head, value)
                slope_ref[:, cols] += dot(head[0:16], slope.astype(BF))
            return carry

        lax.fori_loop(0, tiles, chunk, 0)

    def own_tiles(use):
        for i in range(tiles):
            for j in range(i, tiles):
                use(pl.ds(i * tile, tile), pl.ds(j * tile, tile), i == j)

    def own_near(rows_i, rows_j, diagonal):
        value, slope = matern(dot(a_near[1, rows_i, :], b_own[:, rows_j]), True)
        value, slope = value.astype(BF), slope.astype(BF)
        kbuf[1, rows_i, rows_j] = value
        head = vec[1, :, rows_i]
        acc_k[:, rows_j] += dot(head, value)
        slope_ref[:, rows_j] += dot(head[0:16], slope)
        if not diagonal:
            head = vec[1, :, rows_j]
            acc_k[:, rows_i] += dot_t(head, value)
            slope_ref[:, rows_i] += dot_t(head[0:16], slope)

    a_near[1] = left_side(own, near_scale).T.astype(BF)
    own_tiles(own_near)

    side_scale = far_scale2[:, 0:rank]

    def centred(four):
        full = jnp.concatenate([four, jnp.zeros_like(four)], axis=0)
        return jnp.where(row_ids(full.shape) < 3, full - centre, 0.0)

    arrivals = order[::-1]

    def couplings(batch):
        for level in batch:
            sk[level].wait_recv()
        for level in batch:
            a_side = left_side(centred(prec[level]), side_scale).T.astype(BF)
            b_side = right_side(centred(psel[level]))
            hi, low = split2(matern(dot(a_side, b_side), False))
            chi[level] = hi
            clo[level] = low

    couplings(arrivals[:4])

    valid = [jnp.where(me > 0, 1.0, 0.0), jnp.where(me < n - 1, 1.0, 0.0)]
    for side, slot in ((0, 0), (1, 2)):
        nb[side].wait_recv()
        nb[2 + side].wait_recv()
        p8[0:3, :] = nbp[side]
        a_near[slot] = left_side(p8[...] - centre, near_scale).T.astype(BF)
        hi, low = split2(nbr[side] * valid[side])
        vec[slot, 0:16, :] = hi
        vec[slot, 16:32, :] = low
        vec[slot, 32:48, :] = (marks * valid[side]).astype(BF)
        near_block(slot)

    near_now = acc_k[...]
    sig, noise = sig_ref[0], noise_ref[0]
    rough = noise * r0 + sig * (near_now[0:16] + near_now[16:32] + near_now[32:33] * r0)
    first_a = start_reduce(0, pack([row_dot(r0, r0), row_dot(r0, rough)]))

    couplings(arrivals[4:])

    def mix(copy, received, level, with_ones):
        copy.wait_recv()
        coef = received[level]
        if with_ones:
            tail = jnp.where(row_ids((8, rank)) == 0, prec[level, 3:4, :], 0.0)
            coef = jnp.concatenate([coef, tail], axis=0)
        count = coef.shape[0]
        hi, low = split2(coef)
        both = dot(jnp.concatenate([hi, low], axis=0), chi[level])
        return both[:count] + both[count:] + dot(hi, clo[level])

    def apply_halves(values, matrix):
        total = dot(jnp.concatenate([jnp.concatenate(split2(v), axis=0) for v in values], axis=1), matrix)
        count = total.shape[0] // 2
        return far_scale * (total[:count] + total[count:])

    def far_part(copies, received, with_ones, among):
        sums = [jnp.zeros((24 if with_ones else 16, rank), F32) for _ in range(STRIDE)]
        for level in among:
            mixed = mix(copies[level], received, level, with_ones)
            off = offs[level : level + 1, :]
            for o in range(STRIDE):
                sums[o] = sums[o] + jnp.where(off == o, mixed, 0.0)
        return apply_halves(sums, fbuf[...].reshape(rows, rows))

    far_now = far_part(c1, cr1, True, arrivals)
    near_now = acc_k[...]
    row_sums = near_now[32:33] + far_now[16:17]
    image = noise * r0 + sig * (near_now[0:16] + near_now[16:32] + far_now[0:16] + row_sums * r0)
    slope_image = sig * slope_ref[...]
    slope_ref[...] = slope_image
    q_buf[...] = image
    rs_buf[...] = jnp.broadcast_to(row_sums, rs_buf.shape)
    hi, low = split2(image)
    qvec[1, 0:16, :] = hi
    qvec[1, 16:32, :] = low

    qs = [
        send(qvec.at[1], qvec.at[0], q_send.at[0], q_recv.at[0], right),
        send(qvec.at[1], qvec.at[2], q_send.at[1], q_recv.at[1], left),
    ]

    norm0, start_slope = row_dot(r0, r0), row_dot(r0, slope_image)

    parts = []
    both = dot_t(qvec[1], fbuf[...].reshape(rows, rows))
    for o in range(STRIDE):
        g = both[:, o * rank : (o + 1) * rank]
        parts.append(g[0:16] + g[16:32])
    c2 = {}
    for level in order:
        cs2[level] = choose(level, parts)
        peer = me + flip[level + 1]
        c2[level] = send(cs2.at[level], cr2.at[level], c2_send.at[level], c2_recv.at[level], peer)

    acc_k[...] = jnp.zeros_like(acc_k)

    def own_again(rows_i, rows_j, diagonal):
        value = kbuf[1, rows_i, rows_j]
        acc_k[0:32, rows_j] += dot(qvec[1, :, rows_i], value)
        if not diagonal:
            acc_k[0:32, rows_i] += dot_t(qvec[1, :, rows_j], value)

    own_tiles(own_again)
    acc2 = acc_k[0:32, :]
    first_b = middle_reduce(0, first_a)
    for copy in nb + list(sk.values()) + list(c1.values()):
        copy.wait_send()
    for side, slot in ((0, 0), (1, 2)):
        qs[side].wait_recv()
        acc2 = acc2 + valid[side] * dot(qvec[slot], kbuf[slot])
    last = arrivals[-1]
    column = offs.astype(F32).T[:, last : last + 1]
    picked = jnp.zeros((rank, rows), F32)
    for o in range(STRIDE):
        picked = jnp.where(column == o, fbuf[o].astype(F32), picked)
    basis[...] = picked.astype(BF)
    far_now = far_part(c2, cr2, False, arrivals[:-1])
    image = q_buf[...]
    second = noise * image + sig * (acc2[0:16] + acc2[16:32] + far_now + rs_buf[0:1, :] * image)

    line = end_reduce(0, first_b)
    first_ref[...] = line
    step = unpack(line, 0) / unpack(line, 1)
    slope_image = slope_ref[...]
    r0 = r0_ref[...]
    r1 = r0 - step * image
    r1_ref[...] = r1
    along, square, own_slope = row_dot(r0, r1), row_dot(r1, r1), row_dot(r1, slope_image)
    r1_image = image - step * second
    mixed = mix(c2[last], cr2, last, False)
    r1_image = r1_image - (step * sig) * apply_halves([mixed], basis[...])
    r1_image_ref[...] = r1_image
    line = pack([norm0, along, square, row_dot(r0, r1_image), row_dot(r1, r1_image), start_slope, own_slope])
    second_a = start_reduce(1, line)
    for copy in qs + first_a + list(c2.values()) + first_b:
        copy.wait_send()
    second_b = middle_reduce(1, second_a)
    for copy in second_a:
        copy.wait_send()
    last_ref[...] = end_reduce(1, second_b)
    for copy in second_b:
        copy.wait_send()


def finish(scale, r1_ref, r1_image_ref, q_ref, slope_ref, first_ref, last_ref,
           sol_hbm, res_hbm, slope_hbm, trace_hbm, sol, res, trace_buf, sem):
    outs = [
        pltpu.make_async_copy(src, dst, sem.at[i])
        for i, (src, dst) in enumerate(
            ((slope_ref, slope_hbm), (sol, sol_hbm), (res, res_hbm), (trace_buf, trace_hbm))
        )
    ]
    outs[0].start()
    first, last = first_ref[...], last_ref[...]
    step = unpack(first, 0) / unpack(first, 1)
    norm0, along, square, image_along, image_own, start_slope, own_slope = [unpack(last, k) for k in range(7)]
    share = along / norm0
    gain = norm0 / (norm0 - along)
    inner0 = (norm0 - along) / step
    mixed = (along - square) / step + image_along
    norm1 = gain * gain * (square - share * along)
    inner1 = gain * gain * (image_own - share * mixed + share * share * inner0)
    cross1 = gain * (mixed - 2.0 * share * inner0)
    slope1 = gain * (own_slope - share * start_slope)
    alpha0 = step * gain
    beta = norm1 / norm0
    alpha1 = norm1 / (inner1 + beta * (cross1 + beta * inner0))
    q = q_ref[...]
    r0 = r1_ref[...] + step * q
    r1 = gain * (r1_ref[...] - share * r0)
    sol[...] = (alpha0 + alpha1 * beta) * r0 + alpha1 * r1
    outs[1].start()
    res[...] = r1 - alpha1 * (gain * (r1_image_ref[...] - share * q) + beta * q)
    outs[2].start()
    trace = (alpha0 * start_slope + alpha1 * (slope1 + beta * start_slope)) * scale
    trace_buf[...] = pack([trace])[:, 0:16]
    outs[3].start()
    for out in outs:
        out.wait()


def shards(points, right_sides, skeleton, lengthscale, far_length, signal, noise_var):
    n = lax.axis_size("loc")
    bits = n.bit_length() - 1
    rows = points.shape[1]
    levels, rank = skeleton.shape
    split = min(5, bits // 2 + 1)
    groups = (tuple(range(split)), tuple(range(split, bits)))
    size_a, size_b = 2 ** len(groups[0]), 2 ** len(groups[1])
    vmem = pl.BlockSpec(memory_space=pltpu.VMEM)
    smem = pl.BlockSpec(memory_space=pltpu.SMEM)
    dma = pltpu.SemaphoreType.DMA
    hbm = pl.BlockSpec(memory_space=pltpu.HBM)
    scratch = [
        pltpu.VMEM((3, rows), F32),
        pltpu.VMEM((16, rows), F32),
        pltpu.VMEM((levels, rank), jnp.int32),
        dma((3,)),
        pltpu.VMEM((8, rows), F32),
        pltpu.VMEM((3, VROWS, rows), BF),
        pltpu.VMEM((3, 32, rows), BF),
        pltpu.VMEM((2, 3, rows), F32),
        pltpu.VMEM((2, 16, rows), F32),
        pltpu.VMEM((rows, LANES), F32),
        pltpu.VMEM((3, rows, LANES), BF),
        pltpu.VMEM((STRIDE, rank, LANES), BF),
        pltpu.VMEM((LANES, rows), BF),
        pltpu.VMEM((3, rows, rows), BF),
        pltpu.VMEM((STRIDE, rank, rows), BF),
        pltpu.VMEM((levels, 4, rank), F32),
        pltpu.VMEM((levels, 4, rank), F32),
        pltpu.VMEM((levels, rank, rank), BF),
        pltpu.VMEM((levels, rank, rank), BF),
        pltpu.VMEM((STRIDE, VROWS, rank), F32),
        pltpu.VMEM((levels, 16, rank), F32),
        pltpu.VMEM((levels, 16, rank), F32),
        pltpu.VMEM((levels, 16, rank), F32),
        pltpu.VMEM((levels, 16, rank), F32),
        pltpu.VMEM((VROWS, rows), F32),
        pltpu.VMEM((8, rows), F32),
        pltpu.VMEM((rank, rows), BF),
        pltpu.VMEM((2, size_a, 1, LANES), F32),
        pltpu.VMEM((2, size_b, 1, LANES), F32),
        dma((4,)), dma((4,)), dma((2,)), dma((2,)),
        dma((levels,)), dma((levels,)), dma((levels,)), dma((levels,)), dma((levels,)), dma((levels,)),
        dma((2, size_a - 1)), dma((2, size_a - 1)), dma((2, size_b - 1)), dma((2, size_b - 1)),
    ]
    block = jax.ShapeDtypeStruct(right_sides.shape, F32)
    row = jax.ShapeDtypeStruct((1, LANES), F32)
    parts = pl.pallas_call(
        functools.partial(kernel, bits, groups),
        out_shape=(block,) * 4 + (row,) * 2,
        in_specs=[hbm] * 3 + [smem] * 4,
        out_specs=(vmem,) * 6,
        scratch_shapes=scratch,
        compiler_params=pltpu.CompilerParams(collective_id=0, has_side_effects=True, vmem_limit_bytes=56_200_000),
        name="cg",
    )(*[pltpu.with_memory_space_constraint(a, pltpu.HBM) for a in (points, right_sides, skeleton)], lengthscale, far_length, signal, noise_var)
    probes = right_sides.shape[0]
    outs = pl.pallas_call(
        functools.partial(finish, 1.0 / (n * rows)),
        out_shape=(block, block, block, jax.ShapeDtypeStruct((1, probes), F32)),
        in_specs=[vmem] * 6,
        out_specs=(hbm,) * 4,
        scratch_shapes=[
            pltpu.VMEM(right_sides.shape, F32), pltpu.VMEM(right_sides.shape, F32), pltpu.VMEM((1, probes), F32), dma((4,)),
        ],
        compiler_params=pltpu.CompilerParams(vmem_limit_bytes=2 * 2**20),
        name="finish",
    )(*parts)
    return outs[0], outs[1], outs[2], outs[3].reshape(probes)


def solution(mesh):
    placed = (P(None, "loc"), P(None, "loc"), P(None, "loc"), P(), P(), P(), P())
    return jax.shard_map(
        shards,
        mesh=mesh,
        in_specs=placed,
        out_specs=(P(None, "loc"), P(None, "loc"), P(None, "loc"), P()),
        check_vma=False,
    )
```

```python
import functools

import jax
import jax.numpy as jnp
from jax import lax
from jax.experimental import pallas as pl
from jax.experimental.pallas import tpu as pltpu
from jax.sharding import PartitionSpec as P

F32 = jnp.float32
BF = jnp.bfloat16
LOG2E = 1.4426950408889634
STRIDE = 4
LANES = 128
VROWS = 48
MESH = pl.DeviceIdType.MESH


def split2(x):
    hi = x.astype(BF)
    return hi, (x - hi.astype(F32)).astype(BF)


def split3(x):
    hi = x.astype(BF).astype(F32)
    rest = x - hi
    mid = rest.astype(BF).astype(F32)
    return hi, mid, rest - mid


def row_ids(shape):
    return lax.broadcasted_iota(jnp.int32, shape, 0)


def left_side(pts, scale, extra=None):
    rows = row_ids(pts.shape)
    square = scale * jnp.sum(pts * pts, axis=0, keepdims=True)
    full = jnp.where(rows < 3, -2.0 * scale * pts, jnp.where(rows == 3, square, jnp.where(rows == 4, scale, 0.0)))
    hi, mid, low = split3(full)
    parts = [hi, hi, hi, mid, mid, mid, low, low, low]
    if extra is not None:
        parts.append(extra)
    filler = jnp.zeros((LANES - 8 * len(parts), pts.shape[1]), F32)
    return jnp.concatenate(parts + [filler], axis=0)


def right_side(pts):
    rows = row_ids(pts.shape)
    square = jnp.sum(pts * pts, axis=0, keepdims=True)
    full = jnp.where(rows < 3, pts, jnp.where(rows == 3, 1.0, jnp.where(rows == 4, square, 0.0)))
    hi, mid, low = split3(full)
    filler = jnp.zeros((LANES - 72, pts.shape[1]), F32)
    return jnp.concatenate([hi, mid, low] * 3 + [filler], axis=0).astype(BF)


def matern(square, want_slope):
    square = jnp.maximum(square, 1e-30)
    scaled = square * lax.rsqrt(square)
    decay = jnp.exp2(scaled * (-LOG2E))
    first = scaled * decay
    if want_slope:
        return decay + first, scaled * first
    return decay + first


def dot(a, b):
    return jnp.dot(a, b, preferred_element_type=F32)


def dot_t(a, b):
    return lax.dot_general(a, b, (((1,), (1,)), ((), ())), preferred_element_type=F32)


def pack(columns):
    lanes = lax.broadcasted_iota(jnp.int32, (16, LANES), 1)
    rows = row_ids((16, LANES))
    total = jnp.zeros((16, LANES), F32)
    for k, column in enumerate(columns):
        total = jnp.where(lanes == rows + 16 * k, column, total)
    return jnp.sum(total, axis=0, keepdims=True)


def unpack(line, k):
    lanes = lax.broadcasted_iota(jnp.int32, (16, LANES), 1)
    rows = row_ids((16, LANES))
    return jnp.sum(jnp.where(lanes == rows + 16 * k, line, 0.0), axis=1, keepdims=True)


def row_dot(a, b):
    return jnp.sum(a * b, axis=1, keepdims=True)


def kernel(
    bits, groups, pts_hbm, r0_hbm, skel_hbm, len_ref, far_ref, sig_ref, noise_ref,
    r1_ref, r1_image_ref, q_buf, slope_ref, first_ref, last_ref,
    pts_ref, r0_ref, skel_ref, in_sem, p8, vec, qvec, nbp, nbr, at, a_near, a_far, b_own, kbuf, fbuf, psel, prec, chi, clo, grp,
    cs1, cr1, cs2, cr2, acc_k, rs_buf, basis, red_a, red_b,
    nb_send, nb_recv, q_send, q_recv, sk_send, sk_recv, c1_send, c1_recv, c2_send, c2_recv,
    ra_send, ra_recv, rb_send, rb_recv,
):
    n = 2**bits
    levels, rank = skel_ref.shape
    rows = pts_ref.shape[1]
    tile = rank
    tiles = rows // tile
    far_scale = 1.0 / (rank * rank * levels)
    loads = [
        pltpu.make_async_copy(src, dst, in_sem.at[i])
        for i, (src, dst) in enumerate(((pts_hbm, pts_ref), (skel_hbm, skel_ref), (r0_hbm, r0_ref)))
    ]
    for load in loads:
        load.start()
    me = lax.axis_index("loc")
    flip = [2**b * (1 - 2 * ((me // 2**b) % 2)) for b in range(bits)]
    right = (me + 1) % n
    left = (me + n - 1) % n
    group_a, group_b = groups

    def peers(group):
        found = []
        for d in range(1, 2 ** len(group)):
            found.append(me + sum(flip[b] for i, b in enumerate(group) if (d >> i) & 1))
        return found

    peers_a, peers_b = peers(group_a), peers(group_b)
    barrier = pltpu.get_barrier_semaphore()
    for peer in peers_a[::-1] + peers_b + [left, right]:
        pl.semaphore_signal(barrier, inc=1, device_id=(peer,), device_id_type=MESH)

    def send(src, dst, ssem, rsem, peer):
        copy = pltpu.make_async_remote_copy(
            src_ref=src, dst_ref=dst, send_sem=ssem, recv_sem=rsem, device_id=(peer,), device_id_type=MESH
        )
        copy.start()
        return copy

    def start_reduce(step, line):
        red_a[step, 0] = line
        return [
            send(red_a.at[step, 0], red_a.at[step, d + 1], ra_send.at[step, d], ra_recv.at[step, d], peer)
            for d, peer in enumerate(peers_a)
        ]

    def halve(values):
        while values.shape[0] > 1:
            half = values.shape[0] // 2
            values = values[:half] + values[half:]
        return values[0]

    def middle_reduce(step, copies):
        for copy in copies:
            copy.wait_recv()
        red_b[step, 0] = halve(red_a[step])
        return [
            send(red_b.at[step, 0], red_b.at[step, d + 1], rb_send.at[step, d], rb_recv.at[step, d], peer)
            for d, peer in enumerate(peers_b)
        ]

    def end_reduce(step, copies):
        for copy in copies:
            copy.wait_recv()
        return halve(red_b[step])

    order = sorted(range(levels), key=lambda level: -(2**level if level < 4 else 2 ** (level % 2)))

    p8[...] = jnp.zeros_like(p8)
    loads[0].wait()
    p8[0:3, :] = pts_ref[...]
    raw = p8[...]
    centre = raw[:, 0:1]
    own = raw - centre
    near_scale = 3.0 / jnp.full((1, rows), len_ref[0] * len_ref[0], F32)
    far_scale2 = 3.0 / jnp.full((1, rows), far_ref[0] * far_ref[0], F32)
    b_own[...] = right_side(own)
    at[...] = left_side(own, far_scale2, raw).T
    picks = []
    for o in range(STRIDE):
        part = at[pl.ds(o, rank, stride=STRIDE), :]
        a_far[o] = part.astype(BF)
        picks.append(part.T[72:80, :])

    loads[1].wait()
    offs = skel_ref[...] - STRIDE * lax.broadcasted_iota(jnp.int32, skel_ref.shape, 1)

    def choose(level, values):
        off = offs[level : level + 1, :]
        result = values[0]
        for o in range(1, STRIDE):
            result = jnp.where(off == o, values[o], result)
        return result

    for level in range(levels):
        psel[level, 0:3, :] = choose(level, picks)[0:3]

    loads[2].wait()
    r0 = r0_ref[...]
    hi, low = split2(r0)
    vec[1, 0:16, :] = hi
    vec[1, 16:32, :] = low
    marks = jnp.where(row_ids((16, rows)) == 0, 1.0, 0.0)
    vec[1, 32:48, :] = marks.astype(BF)

    def far_chunk(o, carry):
        left_part = a_far[o]
        for j in range(tiles):
            cols = pl.ds(j * tile, tile)
            fbuf[o, :, cols] = matern(dot(left_part, b_own[:, cols]), False).astype(BF)
        grp[o] = dot_t(vec[1], fbuf[o])
        return carry

    lax.fori_loop(0, STRIDE, far_chunk, 0)

    parts = [grp[o] for o in range(STRIDE)]
    sums = [g[0:16] + g[16:32] for g in parts]
    ones = [g[32:33] for g in parts]
    for level in order:
        cs1[level] = choose(level, sums)
        psel[level, 3:4, :] = choose(level, ones)

    pl.semaphore_wait(barrier, len(peers_a) + len(peers_b) + 2)

    sk, c1 = {}, {}

    def send_coefs(level):
        peer = me + flip[level + 1]
        c1[level] = send(cs1.at[level], cr1.at[level], c1_send.at[level], c1_recv.at[level], peer)

    for i, level in enumerate(order):
        peer = me + flip[level + 1]
        sk[level] = send(psel.at[level], prec.at[level], sk_send.at[level], sk_recv.at[level], peer)
        send_coefs(level)
        if i == min(1, levels - 1):
            nb = [
                send(pts_ref, nbp.at[0], nb_send.at[0], nb_recv.at[0], right),
                send(pts_ref, nbp.at[1], nb_send.at[1], nb_recv.at[1], left),
                send(r0_ref, nbr.at[0], nb_send.at[2], nb_recv.at[2], right),
                send(r0_ref, nbr.at[1], nb_send.at[3], nb_recv.at[3], left),
            ]

    acc_k[...] = jnp.zeros_like(acc_k)
    slope_ref[...] = jnp.zeros_like(slope_ref)

    def near_block(slot):
        def chunk(i, carry):
            at_rows = pl.ds(pl.multiple_of(i * tile, tile), tile)
            left_part = a_near[slot, at_rows, :]
            head = vec[slot, :, at_rows]
            for j in range(tiles):
                cols = pl.ds(j * tile, tile)
                value, slope = matern(dot(left_part, b_own[:, cols]), True)
                value = value.astype(BF)
                kbuf[slot, at_rows, cols] = value
                acc_k[:, cols] += dot(head, value)
                slope_ref[:, cols] += dot(head[0:16], slope.astype(BF))
            return carry

        lax.fori_loop(0, tiles, chunk, 0)

    def own_tiles(use):
        for i in range(tiles):
            for j in range(i, tiles):
                use(pl.ds(i * tile, tile), pl.ds(j * tile, tile), i == j)

    def own_near(rows_i, rows_j, diagonal):
        value, slope = matern(dot(a_near[1, rows_i, :], b_own[:, rows_j]), True)
        value, slope = value.astype(BF), slope.astype(BF)
        kbuf[1, rows_i, rows_j] = value
        head = vec[1, :, rows_i]
        acc_k[:, rows_j] += dot(head, value)
        slope_ref[:, rows_j] += dot(head[0:16], slope)
        if not diagonal:
            head = vec[1, :, rows_j]
            acc_k[:, rows_i] += dot_t(head, value)
            slope_ref[:, rows_i] += dot_t(head[0:16], slope)

    a_near[1] = left_side(own, near_scale).T.astype(BF)
    own_tiles(own_near)

    side_scale = far_scale2[:, 0:rank]

    def centred(four):
        full = jnp.concatenate([four, jnp.zeros_like(four)], axis=0)
        return jnp.where(row_ids(full.shape) < 3, full - centre, 0.0)

    arrivals = order[::-1]

    def couplings(batch):
        for level in batch:
            sk[level].wait_recv()
        for level in batch:
            a_side = left_side(centred(prec[level]), side_scale).T.astype(BF)
            b_side = right_side(centred(psel[level]))
            hi, low = split2(matern(dot(a_side, b_side), False))
            chi[level] = hi
            clo[level] = low

    valid = [jnp.where(me > 0, 1.0, 0.0), jnp.where(me < n - 1, 1.0, 0.0)]
    for side, slot in ((0, 0), (1, 2)):
        nb[side].wait_recv()
        nb[2 + side].wait_recv()
        p8[0:3, :] = nbp[side]
        a_near[slot] = left_side(p8[...] - centre, near_scale).T.astype(BF)
        hi, low = split2(nbr[side] * valid[side])
        vec[slot, 0:16, :] = hi
        vec[slot, 16:32, :] = low
        vec[slot, 32:48, :] = (marks * valid[side]).astype(BF)
        near_block(slot)

    near_now = acc_k[...]
    sig, noise = sig_ref[0], noise_ref[0]
    rough = noise * r0 + sig * (near_now[0:16] + near_now[16:32] + near_now[32:33] * r0)
    first_a = start_reduce(0, pack([row_dot(r0, r0), row_dot(r0, rough)]))

    couplings(arrivals[:4])
    couplings(arrivals[4:])

    def mix(copy, received, level, with_ones):
        copy.wait_recv()
        coef = received[level]
        if with_ones:
            tail = jnp.where(row_ids((8, rank)) == 0, prec[level, 3:4, :], 0.0)
            coef = jnp.concatenate([coef, tail], axis=0)
        count = coef.shape[0]
        hi, low = split2(coef)
        both = dot(jnp.concatenate([hi, low], axis=0), chi[level])
        return both[:count] + both[count:] + dot(hi, clo[level])

    def apply_halves(values, matrix):
        total = dot(jnp.concatenate([jnp.concatenate(split2(v), axis=0) for v in values], axis=1), matrix)
        count = total.shape[0] // 2
        return far_scale * (total[:count] + total[count:])

    def far_part(copies, received, with_ones, among):
        sums = [jnp.zeros((24 if with_ones else 16, rank), F32) for _ in range(STRIDE)]
        for level in among:
            mixed = mix(copies[level], received, level, with_ones)
            off = offs[level : level + 1, :]
            for o in range(STRIDE):
                sums[o] = sums[o] + jnp.where(off == o, mixed, 0.0)
        return apply_halves(sums, fbuf[...].reshape(rows, rows))

    far_now = far_part(c1, cr1, True, arrivals)
    near_now = acc_k[...]
    row_sums = near_now[32:33] + far_now[16:17]
    image = noise * r0 + sig * (near_now[0:16] + near_now[16:32] + far_now[0:16] + row_sums * r0)
    slope_image = sig * slope_ref[...]
    slope_ref[...] = slope_image
    q_buf[...] = image
    rs_buf[...] = jnp.broadcast_to(row_sums, rs_buf.shape)
    hi, low = split2(image)
    qvec[1, 0:16, :] = hi
    qvec[1, 16:32, :] = low

    qs = [
        send(qvec.at[1], qvec.at[0], q_send.at[0], q_recv.at[0], right),
        send(qvec.at[1], qvec.at[2], q_send.at[1], q_recv.at[1], left),
    ]

    norm0, start_slope = row_dot(r0, r0), row_dot(r0, slope_image)

    parts = []
    both = dot_t(qvec[1], fbuf[...].reshape(rows, rows))
    for o in range(STRIDE):
        g = both[:, o * rank : (o + 1) * rank]
        parts.append(g[0:16] + g[16:32])
    c2 = {}
    for level in order:
        cs2[level] = choose(level, parts)
        peer = me + flip[level + 1]
        c2[level] = send(cs2.at[level], cr2.at[level], c2_send.at[level], c2_recv.at[level], peer)

    acc_k[...] = jnp.zeros_like(acc_k)

    def own_again(rows_i, rows_j, diagonal):
        value = kbuf[1, rows_i, rows_j]
        acc_k[0:32, rows_j] += dot(qvec[1, :, rows_i], value)
        if not diagonal:
            acc_k[0:32, rows_i] += dot_t(qvec[1, :, rows_j], value)

    own_tiles(own_again)
    acc2 = acc_k[0:32, :]
    first_b = middle_reduce(0, first_a)
    for copy in nb + list(sk.values()) + list(c1.values()):
        copy.wait_send()
    for side, slot in ((0, 0), (1, 2)):
        qs[side].wait_recv()
        acc2 = acc2 + valid[side] * dot(qvec[slot], kbuf[slot])
    last = arrivals[-1]
    column = offs.astype(F32).T[:, last : last + 1]
    picked = jnp.zeros((rank, rows), F32)
    for o in range(STRIDE):
        picked = jnp.where(column == o, fbuf[o].astype(F32), picked)
    basis[...] = picked.astype(BF)
    far_now = far_part(c2, cr2, False, arrivals[:-1])
    image = q_buf[...]
    second = noise * image + sig * (acc2[0:16] + acc2[16:32] + far_now + rs_buf[0:1, :] * image)

    line = end_reduce(0, first_b)
    first_ref[...] = line
    step = unpack(line, 0) / unpack(line, 1)
    slope_image = slope_ref[...]
    r0 = r0_ref[...]
    r1 = r0 - step * image
    r1_ref[...] = r1
    along, square, own_slope = row_dot(r0, r1), row_dot(r1, r1), row_dot(r1, slope_image)
    r1_image = image - step * second
    mixed = mix(c2[last], cr2, last, False)
    r1_image = r1_image - (step * sig) * apply_halves([mixed], basis[...])
    r1_image_ref[...] = r1_image
    line = pack([norm0, along, square, row_dot(r0, r1_image), row_dot(r1, r1_image), start_slope, own_slope])
    second_a = start_reduce(1, line)
    for copy in qs + first_a + list(c2.values()) + first_b:
        copy.wait_send()
    second_b = middle_reduce(1, second_a)
    for copy in second_a:
        copy.wait_send()
    last_ref[...] = end_reduce(1, second_b)
    for copy in second_b:
        copy.wait_send()


def finish(scale, r1_ref, r1_image_ref, q_ref, slope_ref, first_ref, last_ref,
           sol_hbm, res_hbm, slope_hbm, trace_hbm, sol, res, trace_buf, sem):
    outs = [
        pltpu.make_async_copy(src, dst, sem.at[i])
        for i, (src, dst) in enumerate(
            ((slope_ref, slope_hbm), (sol, sol_hbm), (res, res_hbm), (trace_buf, trace_hbm))
        )
    ]
    outs[0].start()
    first, last = first_ref[...], last_ref[...]
    step = unpack(first, 0) / unpack(first, 1)
    norm0, along, square, image_along, image_own, start_slope, own_slope = [unpack(last, k) for k in range(7)]
    share = along / norm0
    gain = norm0 / (norm0 - along)
    inner0 = (norm0 - along) / step
    mixed = (along - square) / step + image_along
    norm1 = gain * gain * (square - share * along)
    inner1 = gain * gain * (image_own - share * mixed + share * share * inner0)
    cross1 = gain * (mixed - 2.0 * share * inner0)
    slope1 = gain * (own_slope - share * start_slope)
    alpha0 = step * gain
    beta = norm1 / norm0
    alpha1 = norm1 / (inner1 + beta * (cross1 + beta * inner0))
    q = q_ref[...]
    r0 = r1_ref[...] + step * q
    r1 = gain * (r1_ref[...] - share * r0)
    sol[...] = (alpha0 + alpha1 * beta) * r0 + alpha1 * r1
    outs[1].start()
    res[...] = r1 - alpha1 * (gain * (r1_image_ref[...] - share * q) + beta * q)
    outs[2].start()
    trace = (alpha0 * start_slope + alpha1 * (slope1 + beta * start_slope)) * scale
    trace_buf[...] = pack([trace])[:, 0:16]
    outs[3].start()
    for out in outs:
        out.wait()


def shards(points, right_sides, skeleton, lengthscale, far_length, signal, noise_var):
    n = lax.axis_size("loc")
    bits = n.bit_length() - 1
    rows = points.shape[1]
    levels, rank = skeleton.shape
    split = min(5, bits // 2 + 1)
    groups = (tuple(range(split)), tuple(range(split, bits)))
    size_a, size_b = 2 ** len(groups[0]), 2 ** len(groups[1])
    vmem = pl.BlockSpec(memory_space=pltpu.VMEM)
    smem = pl.BlockSpec(memory_space=pltpu.SMEM)
    dma = pltpu.SemaphoreType.DMA
    hbm = pl.BlockSpec(memory_space=pltpu.HBM)
    scratch = [
        pltpu.VMEM((3, rows), F32),
        pltpu.VMEM((16, rows), F32),
        pltpu.VMEM((levels, rank), jnp.int32),
        dma((3,)),
        pltpu.VMEM((8, rows), F32),
        pltpu.VMEM((3, VROWS, rows), BF),
        pltpu.VMEM((3, 32, rows), BF),
        pltpu.VMEM((2, 3, rows), F32),
        pltpu.VMEM((2, 16, rows), F32),
        pltpu.VMEM((rows, LANES), F32),
        pltpu.VMEM((3, rows, LANES), BF),
        pltpu.VMEM((STRIDE, rank, LANES), BF),
        pltpu.VMEM((LANES, rows), BF),
        pltpu.VMEM((3, rows, rows), BF),
        pltpu.VMEM((STRIDE, rank, rows), BF),
        pltpu.VMEM((levels, 4, rank), F32),
        pltpu.VMEM((levels, 4, rank), F32),
        pltpu.VMEM((levels, rank, rank), BF),
        pltpu.VMEM((levels, rank, rank), BF),
        pltpu.VMEM((STRIDE, VROWS, rank), F32),
        pltpu.VMEM((levels, 16, rank), F32),
        pltpu.VMEM((levels, 16, rank), F32),
        pltpu.VMEM((levels, 16, rank), F32),
        pltpu.VMEM((levels, 16, rank), F32),
        pltpu.VMEM((VROWS, rows), F32),
        pltpu.VMEM((8, rows), F32),
        pltpu.VMEM((rank, rows), BF),
        pltpu.VMEM((2, size_a, 1, LANES), F32),
        pltpu.VMEM((2, size_b, 1, LANES), F32),
        dma((4,)), dma((4,)), dma((2,)), dma((2,)),
        dma((levels,)), dma((levels,)), dma((levels,)), dma((levels,)), dma((levels,)), dma((levels,)),
        dma((2, size_a - 1)), dma((2, size_a - 1)), dma((2, size_b - 1)), dma((2, size_b - 1)),
    ]
    block = jax.ShapeDtypeStruct(right_sides.shape, F32)
    row = jax.ShapeDtypeStruct((1, LANES), F32)
    parts = pl.pallas_call(
        functools.partial(kernel, bits, groups),
        out_shape=(block,) * 4 + (row,) * 2,
        in_specs=[hbm] * 3 + [smem] * 4,
        out_specs=(vmem,) * 6,
        scratch_shapes=scratch,
        compiler_params=pltpu.CompilerParams(collective_id=0, has_side_effects=True, vmem_limit_bytes=56_200_000),
        name="cg",
    )(*[pltpu.with_memory_space_constraint(a, pltpu.HBM) for a in (points, right_sides, skeleton)], lengthscale, far_length, signal, noise_var)
    probes = right_sides.shape[0]
    outs = pl.pallas_call(
        functools.partial(finish, 1.0 / (n * rows)),
        out_shape=(block, block, block, jax.ShapeDtypeStruct((1, probes), F32)),
        in_specs=[vmem] * 6,
        out_specs=(hbm,) * 4,
        scratch_shapes=[
            pltpu.VMEM(right_sides.shape, F32), pltpu.VMEM(right_sides.shape, F32), pltpu.VMEM((1, probes), F32), dma((4,)),
        ],
        compiler_params=pltpu.CompilerParams(vmem_limit_bytes=2 * 2**20),
        name="finish",
    )(*parts)
    return outs[0], outs[1], outs[2], outs[3].reshape(probes)


def solution(mesh):
    placed = (P(None, "loc"), P(None, "loc"), P(None, "loc"), P(), P(), P(), P())
    return jax.shard_map(
        shards,
        mesh=mesh,
        in_specs=placed,
        out_specs=(P(None, "loc"), P(None, "loc"), P(None, "loc"), P()),
        check_vma=False,
    )
```
